256 devices in a mesh: seq: 32 (over y, z), head: 8 (over x, core).
Axes of the slice: x: 4, y: 4, z: 8, core: 2. Of those that a mesh axis runs over, the one named last changes fastest.
Arguments:
- queries: bfloat16 [16384, 4096], P('seq', 'head'), may hold values from -8 to 8
- keys: bfloat16 [16384, 4096], P('seq', 'head'), may hold values from -8 to 8
- values: bfloat16 [16384, 4096], P('seq', 'head'), may hold values from -6 to 6
- w_out: bfloat16 [4096, 4096], P('head', 'seq'), may hold values from -0.1875 to 0.1875
- grad_y: bfloat16 [16384, 4096], P('seq', 'head'), may hold values from -6 to 6
Outputs:
- mixer_result: bfloat16 [16384, 4096], P('seq', 'head')
- grad_queries: bfloat16 [16384, 4096], P('seq', 'head')
- grad_keys: bfloat16 [16384, 4096], P('seq', 'head')
- grad_values: bfloat16 [16384, 4096], P('seq', 'head')
- projection_sensitivity: float32 [4096, 4096], P('head', 'seq')
The draws below stay inside these ranges and needn't reach their ends.
All inputs are finite; a program needn't handle non-finite values.
Results may differ from the reference program's by a relative error of at most 0.025.
Values may be sent and summed in bfloat16 or wider, within the bound.
No kernel may reach another device: no remote copies, remote signals or barrier semaphores. Data moves between devices by JAX's collectives and lax.ppermute only.
A program may use at most 128 MiB of HBM per device.

```python
import math
import jax
import jax.numpy as jnp
from jax import lax

H = 32
DH = 128
D = 4096
BLOCK = 64
BAND = 8
TOK_DEV = 512
TOKENS = 16384
N_SEQ = 32
N_HEAD = 8


def pair_rows(key):
    base = jax.random.fold_in(key, 11)
    key_q, key_k = jax.random.split(base, 2)
    query = jnp.clip(jax.random.normal(key_q, (TOKENS, D), jnp.float32), -6.0, 6.0)
    keyed = jnp.clip(jax.random.normal(key_k, (TOKENS, D), jnp.float32), -6.0, 6.0)
    return (query, keyed)


def draw_queries(key, part):
    return pair_rows(key)[0].astype(jnp.bfloat16)


def draw_keys(key, part):
    return pair_rows(key)[1].astype(jnp.bfloat16)


def with_spikes(drawn, own_key, source, target, shards_of, factor):
    def block_of(dim):
        return (jnp.arange(drawn.shape[dim]) // (drawn.shape[dim] // shards_of)).reshape((-1,) + (1,) * (drawn.ndim - 1 - dim))

    one_side = jax.random.permutation(own_key, shards_of)[block_of(target)]
    far = (block_of(target) + shards_of // 2) % shards_of
    return jnp.where((block_of(source) == one_side) | (block_of(source) == far), factor * drawn, drawn)


def steps_of(rng, dims, cuts, low, largest):
    factor_of, own = 1.0, jax.random.fold_in(rng, 6)
    for position, blocks in cuts:
        heights = jnp.exp(jax.random.uniform(jax.random.fold_in(own, position), (blocks,), jnp.float32, low / len(cuts), largest / len(cuts)))
        factor_of = factor_of * jnp.repeat(heights, dims[position] // blocks).reshape([-1 if axis == position else 1 for axis in range(len(dims))])
    return factor_of


def noise(stream_key, shape, scale, bound, pieces=(), kind=jnp.bfloat16):
    values = jax.random.normal(stream_key, shape, jnp.float32) * scale
    if len(pieces) > 0:
        values = steps_of(stream_key, shape, pieces, -0.22, 0.18) * values
    return jnp.clip(values, min=-bound, max=bound).astype(kind)


def gaussian_with(rng, dims, spread, limit, shards, heavy, kind=jnp.bfloat16):
    entries = spread * jax.random.normal(rng, dims, jnp.float32)
    if shards:
        entries = entries * steps_of(rng, dims, shards, -0.22, 0.18)
    return jnp.clip(with_spikes(entries, jax.random.fold_in(rng, 3), *heavy), -limit, limit).astype(kind)


def setup_inputs(seed: int = 0) -> dict:
    arg_keys = jax.random.split(jax.random.key(seed), 6)
    return {
        "queries": draw_queries(jax.random.fold_in(arg_keys[5], 71), 0),
        "keys": draw_keys(jax.random.fold_in(arg_keys[5], 71), 0),
        "values": noise(arg_keys[2], (TOKENS, D), 1.0, 6.0, ((0, 32), (1, 8))),
        "w_out": gaussian_with(arg_keys[3], (D, D), D ** -0.5, 0.1875, ((0, 8), (1, 32)), (0, 1, 32, 2.75)),
        "grad_y": gaussian_with(arg_keys[4], (TOKENS, D), 1.0, 6.0, ((0, 32), (1, 8)), (0, 1, 32, 2.75)),
    }


EPSILON = 1e-05
MASKED = -1e+30

def band_allowed(first, rows, span):
    query = first + jnp.arange(rows, dtype=jnp.int32)
    place = first - (BAND - 1) * BLOCK + jnp.arange(span, dtype=jnp.int32)
    near = place[:, None] // BLOCK >= query[:, None].T // BLOCK - (BAND - 1)
    return (place[:, None] <= query[None, :]) & near & (place[:, None] >= 0)

def score_of(first, q_rows, k_span):
    rows = q_rows.shape[0]
    span = k_span.shape[0]
    score = jnp.dot(k_span, q_rows.T, preferred_element_type=jnp.float32) * (1.0 / math.sqrt(DH))
    return jnp.where(band_allowed(first, rows, span), score, MASKED)

def linear_forward(q_head, k_head, v_head):
    block_count = q_head.shape[0] // BLOCK
    query_block_rows = q_head.reshape(block_count, BLOCK, DH).astype(jnp.float32)
    lookup_tile_entries = k_head.reshape(block_count, BLOCK, DH).astype(jnp.float32)
    value_block_rows = v_head.reshape(block_count, BLOCK, DH).astype(jnp.float32)
    cross_block_totals = jnp.einsum('mpl,mpw->mlw', lookup_tile_entries, value_block_rows)
    running_state = (jnp.cumsum(cross_block_totals, axis=0) - cross_block_totals).astype(jnp.bfloat16)
    causal = jnp.arange(BLOCK)[:, None] >= jnp.arange(BLOCK)[None, :]
    inside_block_scores = jnp.where(causal, jnp.einsum('ntk,njk->ntj', query_block_rows, lookup_tile_entries), 0.0).astype(jnp.bfloat16)
    linear_branch = jnp.einsum('wqf,wfa->wqa', query_block_rows, running_state.astype(jnp.float32))
    linear_branch = linear_branch + jnp.einsum('ntj,njv->ntv', inside_block_scores.astype(jnp.float32), value_block_rows)
    linear_branch = linear_branch.reshape(-1, DH)
    inv_rms = lax.rsqrt(lax.optimization_barrier(jnp.mean(linear_branch * linear_branch, axis=-1, keepdims=True)) + EPSILON)
    return (running_state, inside_block_scores, linear_branch * inv_rms, inv_rms)

def window_forward(q_head, k_head, v_head):
    rows = BAND * BLOCK
    edge = (BAND - 1) * BLOCK
    span = rows + edge
    length = q_head.shape[0]
    k_wide = jnp.concatenate([jnp.zeros((edge, DH), k_head.dtype), k_head])
    v_wide = jnp.concatenate([jnp.zeros((edge, DH), v_head.dtype), v_head])

    def one_block(index):
        first = index * rows
        q_rows = lax.dynamic_slice_in_dim(q_head, first, rows, 0)
        k_span = lax.dynamic_slice_in_dim(k_wide, first, span, 0)
        v_span = lax.dynamic_slice_in_dim(v_wide, first, span, 0)
        score = score_of(first, q_rows, k_span)
        row_max = lax.optimization_barrier(jnp.max(score, axis=0))
        raised = jnp.exp(score - row_max[None, :])
        inv_total = 1.0 / lax.optimization_barrier(jnp.sum(raised, axis=0))
        probs = (raised * inv_total[None, :]).astype(jnp.bfloat16)
        return (jnp.dot(probs.T, v_span, preferred_element_type=jnp.float32), row_max, inv_total)
    outs, row_max, inv_total = lax.map(one_block, jnp.arange(length // rows, dtype=jnp.int32))
    return (outs.reshape(length, DH), row_max, inv_total, k_wide, v_wide)

def head_mixed(parts):
    q_head, k_head, v_head = parts
    running_state, inside_block_scores, normed, inv_rms = linear_forward(q_head, k_head, v_head)
    window, row_max, inv_total, k_wide, v_wide = window_forward(q_head, k_head, v_head)
    return (normed + window).astype(jnp.bfloat16)

def head_backward(parts):
    q_head, k_head, v_head, grad_head = parts
    length = q_head.shape[0]
    rows = BAND * BLOCK
    edge = (BAND - 1) * BLOCK
    span = rows + edge
    score_scale = 1.0 / math.sqrt(DH)
    running_state, inside_block_scores, normed, inv_rms = linear_forward(q_head, k_head, v_head)
    window, row_max, inv_total, k_wide, v_wide = window_forward(q_head, k_head, v_head)
    grad_f = grad_head.astype(jnp.float32)
    delta = lax.optimization_barrier(jnp.sum(grad_f * window, axis=-1))
    inner = lax.optimization_barrier(jnp.mean(grad_f * normed, axis=-1, keepdims=True))
    grad_lin = (inv_rms * (grad_f - normed * inner)).astype(jnp.bfloat16)
    block_count = length // BLOCK
    query_block_rows = q_head.reshape(block_count, BLOCK, DH).astype(jnp.float32)
    lookup_tile_entries = k_head.reshape(block_count, BLOCK, DH).astype(jnp.float32)
    value_block_rows = v_head.reshape(block_count, BLOCK, DH).astype(jnp.float32)
    upstream_tile_entries = grad_lin.reshape(block_count, BLOCK, DH).astype(jnp.float32)
    reverse_state_totals = jnp.einsum('xlm,xla->xma', query_block_rows, upstream_tile_entries)
    back_state = (lax.optimization_barrier(jnp.sum(reverse_state_totals, axis=0))[None] - jnp.cumsum(reverse_state_totals, axis=0)).astype(jnp.bfloat16)
    causal = jnp.arange(BLOCK)[:, None] >= jnp.arange(BLOCK)[None, :]
    intra_grad = jnp.where(causal, jnp.einsum('ntv,njv->ntj', upstream_tile_entries, value_block_rows), 0.0).astype(jnp.bfloat16)
    cumulative_memory_single = running_state.astype(jnp.float32)
    reverse_state_float = back_state.astype(jnp.float32)
    local_derivative_single = intra_grad.astype(jnp.float32)
    asking_plain_entries = jnp.einsum('nrq,nhq->nrh', upstream_tile_entries, cumulative_memory_single) + jnp.einsum('wri,wid->wrd', local_derivative_single, lookup_tile_entries)
    key_linear_rows = jnp.einsum('lou,leu->loe', value_block_rows, reverse_state_float) + jnp.einsum('uda,udr->uar', local_derivative_single, query_block_rows)
    value_linear_rows = jnp.einsum('uwb,ubc->uwc', lookup_tile_entries, reverse_state_float) + jnp.einsum('owu,owh->ouh', inside_block_scores.astype(jnp.float32), upstream_tile_entries)

    def one_back(index, carry):
        q_acc, k_acc, v_acc = carry
        first = (index * rows).astype(jnp.int32)
        q_rows = lax.dynamic_slice_in_dim(q_head, first, rows, 0)
        k_span = lax.dynamic_slice_in_dim(k_wide, first, span, 0)
        v_span = lax.dynamic_slice_in_dim(v_wide, first, span, 0)
        grad_rows = lax.dynamic_slice_in_dim(grad_head, first, rows, 0)
        score = score_of(first, q_rows, k_span)
        probs = (jnp.exp(score - row_max[index][None, :]) * inv_total[index][None, :]).astype(jnp.bfloat16)
        dprob = jnp.dot(v_span, grad_rows.T, preferred_element_type=jnp.float32)
        delta_rows = lax.dynamic_slice_in_dim(delta, first, rows, 0)
        dscore = (probs.astype(jnp.float32) * (dprob - delta_rows[None, :]) * score_scale).astype(jnp.bfloat16)
        q_acc = lax.dynamic_update_slice_in_dim(q_acc, jnp.dot(dscore.T, k_span, preferred_element_type=jnp.float32), first, 0)
        k_new = lax.dynamic_slice_in_dim(k_acc, first, span, 0) + jnp.dot(dscore, q_rows, preferred_element_type=jnp.float32)
        v_new = lax.dynamic_slice_in_dim(v_acc, first, span, 0) + jnp.dot(probs, grad_rows, preferred_element_type=jnp.float32)
        k_acc = lax.dynamic_update_slice_in_dim(k_acc, k_new, first, 0)
        v_acc = lax.dynamic_update_slice_in_dim(v_acc, v_new, first, 0)
        return (q_acc, k_acc, v_acc)
    start_carry = (jnp.zeros((length, DH), jnp.float32), jnp.zeros((length + edge, DH), jnp.float32), jnp.zeros((length + edge, DH), jnp.float32))
    q_window, k_window, v_window = lax.fori_loop(0, length // rows, one_back, start_carry)
    grad_q = (asking_plain_entries.reshape(length, DH) + q_window).astype(jnp.bfloat16)
    grad_k = (key_linear_rows.reshape(length, DH) + k_window[edge:]).astype(jnp.bfloat16)
    grad_v = (value_linear_rows.reshape(length, DH) + v_window[edge:]).astype(jnp.bfloat16)
    return (grad_q, grad_k, grad_v)

def reference(queries, keys, values, w_out, grad_y):
    length = queries.shape[0]

    def by_head(array):
        return array.reshape(length, H, DH).transpose(1, 0, 2)

    def by_token(array):
        return array.transpose(1, 0, 2).reshape(length, D)
    heads = (by_head(queries), by_head(keys), by_head(values))
    mixed = by_token(lax.map(head_mixed, heads))
    group_width = H // N_HEAD * DH
    layer_total = jnp.zeros((length, D), jnp.float32)
    for group in range(N_HEAD):
        low = group * group_width
        part_sum = jnp.dot(mixed[:, low:low + group_width], w_out[low:low + group_width], preferred_element_type=jnp.float32).astype(jnp.bfloat16)
        layer_total = layer_total + lax.optimization_barrier(part_sum).astype(jnp.float32)
    mixer_result = layer_total.astype(jnp.bfloat16)
    grad_mixed = lax.dot_general(grad_y, w_out, (((1,), (1,)), ((), ())), preferred_element_type=jnp.float32).astype(jnp.bfloat16)

    def add_run(index, total):
        first = (index * TOK_DEV).astype(jnp.int32)
        mixed_run = lax.dynamic_slice_in_dim(mixed, first, TOK_DEV, 0)
        grad_run = lax.dynamic_slice_in_dim(grad_y, first, TOK_DEV, 0)
        term = lax.dot_general(mixed_run, grad_run, (((0,), (0,)), ((), ())), preferred_element_type=jnp.float32).astype(jnp.bfloat16)
        return total + lax.optimization_barrier(term).astype(jnp.float32)
    grad_total = lax.fori_loop(0, N_SEQ, add_run, jnp.zeros((D, D), jnp.float32))
    projection_sensitivity = grad_total * TOKENS ** (-0.5)
    grad_q, grad_k, grad_v = lax.map(head_backward, heads + (by_head(grad_mixed),))
    return (mixer_result, by_token(grad_q), by_token(grad_k), by_token(grad_v), projection_sensitivity)
```

```python
import functools
import math

import jax
import jax.numpy as jnp
from jax import lax
from jax.experimental import pallas as pl
from jax.experimental.pallas import tpu as pltpu
from jax.sharding import PartitionSpec as P

DH = 128
BLOCK = 64
BAND = 8
TILE = 128
TOK = BAND * BLOCK
EDGE = TOK - BLOCK
SCALE = 1.0 / math.sqrt(DH)
EPSILON = 1e-05
MASKED = -1e30
F32 = jnp.float32
BF16 = jnp.bfloat16


def nn(a, b):
    return lax.dot_general(a, b, (((1,), (0,)), ((), ())), preferred_element_type=F32)


def nt(a, b):
    return lax.dot_general(a, b, (((1,), (1,)), ((), ())), preferred_element_type=F32)


def tn(a, b):
    return lax.dot_general(a, b, (((0,), (0,)), ((), ())), preferred_element_type=F32)


def flip(a):
    return a.astype(F32).T


def call(kernel, heads, ins, outs, out_shape, scratch=(), flops=0, size=0, prefetch=0):
    return pl.pallas_call(
        kernel,
        grid_spec=pltpu.PrefetchScalarGridSpec(
            num_scalar_prefetch=prefetch,
            grid=(heads,),
            in_specs=ins,
            out_specs=outs,
            scratch_shapes=scratch,
        ),
        out_shape=out_shape,
        compiler_params=pltpu.CompilerParams(
            dimension_semantics=("arbitrary",), vmem_limit_bytes=48 * 1024 * 1024
        ),
        cost_estimate=pl.CostEstimate(flops=flops, bytes_accessed=size, transcendentals=0),
    )


def columns(rows, at=0):
    return pl.BlockSpec((rows, DH), lambda h, *_: (at, h))


def heads_of(*dims):
    return pl.BlockSpec((1,) + dims, lambda h, *_: (h,) + (0,) * len(dims))


def rows_of(rows, cols):
    return pl.BlockSpec((rows, cols), lambda h, *_: (h, 0))


def sums_kernel(k, v, out):
    out[0] = tn(k[...], v[...]).astype(BF16)


def causal_tile():
    row = lax.broadcasted_iota(jnp.int32, (TILE, TILE), 0)
    col = lax.broadcasted_iota(jnp.int32, (TILE, TILE), 1)
    return row <= col


def edge_tile():
    row = lax.broadcasted_iota(jnp.int32, (TILE, TILE), 0)
    col = lax.broadcasted_iota(jnp.int32, (TILE, TILE), 1)
    return (row >= BLOCK) & (col < BLOCK)


def pad_into(wide, part):
    wide[0:BLOCK, :] = jnp.zeros((BLOCK, DH), BF16)
    wide[BLOCK:TOK, :] = part[...]


def window_kernel(place, q, k, v, kh, vh, near, far, raw, window, intra, kw, vw):
    pad_into(kw, kh)
    pad_into(vw, vh)
    causal, edge = causal_tile(), edge_tile()
    inside = place[0] > 0
    v_t = flip(v[...]).astype(BF16)
    vh_t = flip(vw[...]).astype(BF16)
    for i in range(TOK // TILE):
        lo, hi = i * TILE, (i + 1) * TILE
        q_i = q[lo:hi, :]
        s_near = nt(k[0:hi, :], q_i)
        s_far = nt(kw[lo:TOK, :], q_i) * SCALE
        if i == 0:
            s_near = jnp.where(causal, s_near, 0.0)
            raw_i = s_near.astype(BF16)
            s_near = jnp.where(causal, s_near * SCALE, MASKED)
        else:
            full, last = s_near[0:lo], s_near[lo:hi]
            raw_i = jnp.concatenate([full, jnp.where(causal, last, 0.0)]).astype(BF16)
            s_near = jnp.concatenate([full * SCALE, jnp.where(causal, last * SCALE, MASKED)])
        raw[0, 0:hi, lo:hi] = raw_i
        head = jnp.where(edge, s_far[0:TILE], MASKED)
        if i < TOK // TILE - 1:
            s_far = jnp.concatenate([head, s_far[TILE:]])
        else:
            s_far = head
        s_far = jnp.where(inside, s_far, MASKED)
        top = jnp.maximum(
            jnp.max(s_near, axis=0, keepdims=True), jnp.max(s_far, axis=0, keepdims=True)
        )
        p_near = jnp.exp(s_near - top)
        p_far = jnp.exp(s_far - top)
        inv = 1.0 / (
            jnp.sum(p_near, axis=0, keepdims=True) + jnp.sum(p_far, axis=0, keepdims=True)
        )
        p_near = (p_near * inv).astype(BF16)
        p_far = (p_far * inv).astype(BF16)
        near[0, 0:hi, lo:hi] = p_near
        far[0, lo:TOK, lo:hi] = p_far
        window[:, lo:hi] = nn(v_t[:, 0:hi], p_near) + nn(vh_t[:, lo:TOK], p_far)
        intra[:, lo:hi] = nn(v_t[:, 0:hi], raw_i)


def mixed_kernel(q, before, window, intra, normed, inverse, mixed_t, mixed):
    lin = intra[...] + nt(flip(before[0]).astype(BF16), q[...])
    inv = lax.rsqrt(jnp.mean(lin * lin, axis=0, keepdims=True) + EPSILON)
    unit = lin * inv
    normed[...] = unit
    inverse[0] = inv
    out = unit + window[...]
    mixed_t[...] = out.astype(BF16)
    mixed[...] = out.T.astype(BF16)


def far_kernel(q, g, kh, vh, far, window, dq, dk, dv, delta, kw, vw, ds):
    pad_into(kw, kh)
    pad_into(vw, vh)
    g_t = flip(g[...])
    d = jnp.sum(g_t * window[...], axis=0, keepdims=True)
    delta[0] = d
    kh_t = flip(kw[...]).astype(BF16)
    for i in range(TOK // TILE):
        lo, hi = i * TILE, (i + 1) * TILE
        dp = nt(vw[lo:TOK, :], g[lo:hi, :])
        part = (far[0, lo:TOK, lo:hi].astype(F32) * (dp - d[:, lo:hi]) * SCALE).astype(BF16)
        ds[lo:TOK, lo:hi] = part
        dq[:, lo:hi] = nn(kh_t[:, lo:TOK], part)
    for j in range(TOK // TILE):
        lo, hi = j * TILE, (j + 1) * TILE
        dk_j = nn(ds[lo:hi, 0:hi], q[0:hi, :]).astype(BF16)
        dv_j = nn(far[0, lo:hi, 0:hi], g[0:hi, :]).astype(BF16)
        if j == 0:
            dk[0 : hi - BLOCK, :] = dk_j[BLOCK:]
            dv[0 : hi - BLOCK, :] = dv_j[BLOCK:]
        else:
            dk[lo - BLOCK : hi - BLOCK, :] = dk_j
            dv[lo - BLOCK : hi - BLOCK, :] = dv_j


def lin_kernel(q, g, normed, inverse, grad_lin, sums):
    g_t = flip(g[...])
    unit = normed[...]
    inner = jnp.mean(g_t * unit, axis=0, keepdims=True)
    out = inverse[0] * (g_t - unit * inner)
    rows = out.T.astype(BF16)
    grad_lin[...] = rows
    sums[0] = tn(q[...], rows).astype(BF16)


def near_kernel(q, k, v, g, gl, near, raw, before, delta, dq_far, dq, dk, dv, both):
    causal = causal_tile()
    d = delta[0]
    k_t = flip(k[...]).astype(BF16)
    dq_t = dq_far[...] + nt(before[0], gl[...])
    parts = []
    for i in range(TOK // TILE):
        lo, hi = i * TILE, (i + 1) * TILE
        dp = nt(v[0:hi, :], g[lo:hi, :])
        ig = nt(v[0:hi, :], gl[lo:hi, :])
        last = jnp.where(causal, ig[lo:hi], 0.0)
        ig = last if i == 0 else jnp.concatenate([ig[0:lo], last])
        sum_i = near[0, 0:hi, lo:hi].astype(F32) * (dp - d[:, lo:hi]) * SCALE + ig
        sum_i = sum_i.astype(BF16)
        both[0:hi, lo:hi] = sum_i
        parts.append(dq_t[:, lo:hi] + nn(k_t[:, 0:hi], sum_i))
    dq[...] = jnp.concatenate(parts, axis=1).T.astype(BF16)
    for j in range(TOK // TILE):
        lo, hi = j * TILE, (j + 1) * TILE
        dk[lo:hi, :] = nn(both[lo:hi, lo:TOK], q[lo:TOK, :])
        dv[lo:hi, :] = nn(near[0, lo:hi, lo:TOK], g[lo:TOK, :]) + nn(
            raw[0, lo:hi, lo:TOK], gl[lo:TOK, :]
        )


def last_kernel(k, v, later, dk, dv, rk, rv, out_k, out_v):
    state = later[0]
    add_k = dk[...] + nt(v[...], state)
    add_v = dv[...] + nn(k[...], state)
    out_k[0:BLOCK, :] = add_k[0:BLOCK].astype(BF16)
    out_v[0:BLOCK, :] = add_v[0:BLOCK].astype(BF16)
    out_k[BLOCK:TOK, :] = (add_k[BLOCK:] + rk[...].astype(F32)).astype(BF16)
    out_v[BLOCK:TOK, :] = (add_v[BLOCK:] + rv[...].astype(F32)).astype(BF16)


def scan_kernel(backward, x, out):
    total = jnp.zeros(x.shape[1:], F32)
    count = x.shape[0]
    for i in range(count):
        at = count - 1 - i if backward else i
        out[at] = total.astype(BF16)
        total = total + x[at].astype(F32)


def carry_states(local, backward):
    count = lax.axis_size("seq")
    pieces = local.reshape(count, -1, DH)
    met = lax.all_to_all(pieces, "seq", 0, 0)
    done = pl.pallas_call(
        functools.partial(scan_kernel, backward),
        out_shape=jax.ShapeDtypeStruct(met.shape, BF16),
    )(met)
    return lax.all_to_all(done, "seq", 0, 0).reshape(local.shape)


def whole(kernel, ids, ins, out_shape, scratch=(), flops=0, size=0):
    vmem = pl.BlockSpec(memory_space=pltpu.VMEM)
    smem = pl.BlockSpec(memory_space=pltpu.SMEM)
    return pl.pallas_call(
        kernel,
        in_specs=[smem] + [vmem] * len(ins),
        out_specs=jax.tree.map(lambda _: vmem, out_shape),
        out_shape=out_shape,
        scratch_shapes=scratch,
        compiler_params=pltpu.CompilerParams(vmem_limit_bytes=48 * 1024 * 1024),
        cost_estimate=pl.CostEstimate(flops=flops, bytes_accessed=size, transcendentals=0),
    )(ids, *ins)


def grad_mixed_kernel(ids, w, *rest):
    blocks, out, acc = rest[:-2], rest[-2], rest[-1]
    width = blocks[0].shape[1]
    for j, block in enumerate(blocks):
        at = pl.multiple_of(ids[j] * width, width)
        part = nt(block[...], w[:, pl.ds(at, width)])
        if j == 0:
            acc[...] = part
        elif j < len(blocks) - 1:
            acc[...] += part
        else:
            out[...] = (acc[...] + part).astype(BF16)


def sens_kernel(n, ids, mixed_t, *rest):
    blocks, outs = rest[:n], rest[n:]
    width = blocks[0].shape[1]
    for j, block in enumerate(blocks):
        part = nn(mixed_t[...], block[...]).astype(BF16)
        slot, at = ids[n + j], pl.multiple_of(ids[2 * n + j] * width, width)
        for r, out in enumerate(outs):

            @pl.when(slot == r)
            def _(out=out, part=part, at=at):
                out[:, pl.ds(at, width)] = part


def fold_kernel(n, ids, *rest):
    parts, outs = rest[:n], rest[n:]
    width = outs[0].shape[1]
    for j, out in enumerate(outs):
        at = pl.ds(pl.multiple_of(ids[j] * width, width), width)
        total = parts[0][:, at].astype(F32)
        for part in parts[1:]:
            total = total + part[:, at].astype(F32)
        out[...] = total.astype(BF16)


YS, ZS, XS = 4, 8, 4
Y_HOPS = (1, 3, 2)
Z_HOPS = (1, 7, 2, 6, 3, 5, 4)


def shifted(shard, by):
    count = lax.axis_size("seq")
    pairs = [(i, i + by) for i in range(count) if 0 <= i + by < count]
    return lax.ppermute(shard, "seq", pairs)


def hop_y(shard, by):
    return lax.ppermute(
        shard, "seq", [(y * ZS + z, (y + by) % YS * ZS + z) for y in range(YS) for z in range(ZS)]
    )


def hop_z(shard, by):
    return lax.ppermute(
        shard, "seq", [(y * ZS + z, y * ZS + (z + by) % ZS) for y in range(YS) for z in range(ZS)]
    )


def hop_x(shard, by):
    return lax.ppermute(
        shard, "head", [(x * 2 + c, (x + by) % XS * 2 + c) for x in range(XS) for c in range(2)]
    )


def swap_core(shard):
    return lax.ppermute(shard, "head", [(i, i ^ 1) for i in range(2 * XS)])


def shards(queries, keys, values, w_out, grad_y):
    rows, width = queries.shape
    heads = width // DH
    seq, head = lax.axis_index("seq"), lax.axis_index("head")
    y, z, x, core = seq // ZS, seq % ZS, head // 2, head % 2
    tokens_all = rows * lax.axis_size("seq")
    shape = jax.ShapeDtypeStruct
    col = columns(rows)
    tri = heads_of(rows, rows)
    st = heads_of(DH, DH)
    turned = rows_of(DH, rows)
    line = heads_of(1, rows)
    mm = 2 * rows * rows * width

    halo = shifted(jnp.concatenate([keys[BLOCK:], values[BLOCK:]]), 1)
    full_w = lax.all_gather(w_out, "seq", axis=1, tiled=True)
    grads = [grad_y] + [hop_x(grad_y, by) for by in (1, XS - 1, 2)]
    grads = grads + [swap_core(g) for g in grads]
    source = [(x - by) % XS for by in (0, 1, XS - 1, 2)]
    block_of = [s * 2 + core for s in source] + [s * 2 + 1 - core for s in source]
    slot_of = [(b // 2 - y) % YS for b in block_of]
    ids = jnp.stack(block_of + slot_of + [b % 2 for b in block_of]).astype(jnp.int32)

    local = call(
        sums_kernel, heads, [col, col], st, shape((heads, DH, DH), BF16), flops=2 * mm // 4
    )(keys, values)
    before = carry_states(local, False)

    sq = shape((heads, rows, rows), BF16)
    flat_t = shape((width, rows), F32)
    edge = EDGE
    wide = [pltpu.VMEM((rows, DH), BF16)] * 2
    near, far, raw, window, intra = call(
        window_kernel,
        heads,
        [col, col, col, columns(edge, 0), columns(edge, 1)],
        [tri, tri, tri, turned, turned],
        [sq, sq, sq, flat_t, flat_t],
        scratch=wide,
        flops=12 * mm // 8,
        size=12 << 20,
        prefetch=1,
    )(seq.reshape(1).astype(jnp.int32), queries, keys, values, halo, halo)

    normed, inverse, mixed_t, mixed = call(
        mixed_kernel,
        heads,
        [col, st, turned, turned],
        [turned, line, turned, col],
        [
            flat_t,
            shape((heads, 1, rows), F32),
            shape((width, rows), BF16),
            shape((rows, width), BF16),
        ],
        flops=mm // 4,
        size=5 << 20,
    )(queries, before, window, intra)

    pieces = whole(
        functools.partial(sens_kernel, len(grads)),
        ids,
        [mixed_t] + grads,
        [shape((width, 2 * width), BF16)] * YS,
        flops=8 * mm,
        size=9 << 20,
    )
    got = [pieces[0]] + [hop_y(pieces[by], by) for by in Y_HOPS]
    z_ids = jnp.stack([(z + by) % ZS for by in (0,) + Z_HOPS]).astype(jnp.int32)
    parts = whole(
        functools.partial(fold_kernel, YS),
        z_ids,
        got,
        [shape((width, DH), BF16)] * ZS,
        size=5 << 20,
    )
    total = parts[0].astype(F32)
    for part, by in zip(parts[1:], Z_HOPS):
        total = total + hop_z(part, by).astype(F32)
    projection_sensitivity = total * tokens_all ** (-0.5)

    grad_mixed = whole(
        grad_mixed_kernel,
        ids,
        [full_w] + grads,
        shape((rows, width), BF16),
        scratch=[pltpu.VMEM((rows, width), F32)],
        flops=8 * mm,
        size=9 << 20,
    )
    partial_value = jnp.dot(mixed, full_w, preferred_element_type=F32).astype(BF16)
    mixer_result = lax.psum_scatter(partial_value, "head", scatter_dimension=1, tiled=True)

    edge_grad = shape((edge, width), BF16)
    dq_far, far_k, far_v, delta = call(
        far_kernel,
        heads,
        [col, col, columns(edge, 0), columns(edge, 1), tri, turned],
        [turned, columns(edge), columns(edge), line],
        [flat_t, edge_grad, edge_grad, shape((heads, 1, rows), F32)],
        scratch=wide + [pltpu.VMEM((rows, rows), BF16)],
        flops=8 * mm // 8,
        size=8 << 20,
    )(queries, grad_mixed, halo, halo, far, window)
    back_k, back_v = shifted(far_k, -1), shifted(far_v, -1)

    grad_lin, local_back = call(
        lin_kernel,
        heads,
        [col, col, turned, line],
        [col, st],
        [shape((rows, width), BF16), shape((heads, DH, DH), BF16)],
        flops=mm // 4,
        size=3 << 20,
    )(queries, grad_mixed, normed, inverse)
    later = carry_states(local_back, True)

    grad_queries, near_k, near_v = call(
        near_kernel,
        heads,
        [col, col, col, col, col, tri, tri, st, line, turned],
        [col, col, col],
        [shape((rows, width), BF16), shape((rows, width), F32), shape((rows, width), F32)],
        scratch=[pltpu.VMEM((rows, rows), BF16)],
        flops=12 * mm // 8,
        size=12 << 20,
    )(queries, keys, values, grad_mixed, grad_lin, near, raw, before, delta, dq_far)

    grad_keys, grad_values = call(
        last_kernel,
        heads,
        [col, col, st, col, col, columns(edge), columns(edge)],
        [col, col],
        [shape((rows, width), BF16)] * 2,
        flops=mm // 2,
        size=5 << 20,
    )(keys, values, later, near_k, near_v, back_k, back_v)
    return (mixer_result, grad_queries, grad_keys, grad_values, projection_sensitivity)


def solution(mesh):
    placed = (
        P("seq", "head"),
        P("seq", "head"),
        P("seq", "head"),
        P("head", "seq"),
        P("seq", "head"),
    )
    return jax.shard_map(
        shards,
        mesh=mesh,
        in_specs=placed,
        out_specs=(
            P("seq", "head"),
            P("seq", "head"),
            P("seq", "head"),
            P("seq", "head"),
            P("head", "seq"),
        ),
        check_vma=False,
    )
```

```python
import functools
import math

import jax
import jax.numpy as jnp
from jax import lax
from jax.experimental import pallas as pl
from jax.experimental.pallas import tpu as pltpu
from jax.sharding import PartitionSpec as P

DH = 128
BLOCK = 64
BAND = 8
TILE = 128
TOK = BAND * BLOCK
EDGE = TOK - BLOCK
SCALE = 1.0 / math.sqrt(DH)
EPSILON = 1e-05
MASKED = -1e30
F32 = jnp.float32
BF16 = jnp.bfloat16


def nn(a, b):
    return lax.dot_general(a, b, (((1,), (0,)), ((), ())), preferred_element_type=F32)


def nt(a, b):
    return lax.dot_general(a, b, (((1,), (1,)), ((), ())), preferred_element_type=F32)


def tn(a, b):
    return lax.dot_general(a, b, (((0,), (0,)), ((), ())), preferred_element_type=F32)


def flip(a):
    return a.astype(F32).T


def call(kernel, heads, ins, outs, out_shape, scratch=(), flops=0, size=0, prefetch=0):
    run = pl.pallas_call(
        kernel,
        grid_spec=pltpu.PrefetchScalarGridSpec(
            num_scalar_prefetch=prefetch,
            grid=(heads,),
            in_specs=ins,
            out_specs=outs,
            scratch_shapes=scratch,
        ),
        out_shape=out_shape,
        compiler_params=pltpu.CompilerParams(
            dimension_semantics=("arbitrary",), vmem_limit_bytes=40 * 1024 * 1024
        ),
        cost_estimate=pl.CostEstimate(flops=flops, bytes_accessed=size, transcendentals=0),
    )
    return lambda *args: run(*args[:prefetch], *(kept(a) for a in args[prefetch:]))


def kept(a):
    return pltpu.with_memory_space_constraint(a, pltpu.HBM)


def large(*args):
    return pltpu.HBM(*args)


def columns(rows, at=0):
    return pl.BlockSpec((rows, DH), lambda h, *_: (at, h))


def heads_of(*dims):
    return pl.BlockSpec((1,) + dims, lambda h, *_: (h,) + (0,) * len(dims))


def rows_of(rows, cols):
    return pl.BlockSpec((rows, cols), lambda h, *_: (h, 0))


def sums_kernel(k, v, out):
    out[0] = tn(k[...], v[...]).astype(BF16)


def causal_tile():
    row = lax.broadcasted_iota(jnp.int32, (TILE, TILE), 0)
    col = lax.broadcasted_iota(jnp.int32, (TILE, TILE), 1)
    return row <= col


def edge_tile():
    row = lax.broadcasted_iota(jnp.int32, (TILE, TILE), 0)
    col = lax.broadcasted_iota(jnp.int32, (TILE, TILE), 1)
    return (row >= BLOCK) & (col < BLOCK)


def window_kernel(place, q, k, v, kw, vw, near, far, raw, window, intra):
    causal, edge = causal_tile(), edge_tile()
    inside = place[0] > 0
    v_t = flip(v[...]).astype(BF16)
    vh_t = flip(vw[...]).astype(BF16)
    for i in range(TOK // TILE):
        lo, hi = i * TILE, (i + 1) * TILE
        q_i = q[lo:hi, :]
        s_near = nt(k[0:hi, :], q_i)
        s_far = nt(kw[lo:TOK, :], q_i) * SCALE
        if i == 0:
            s_near = jnp.where(causal, s_near, 0.0)
            raw_i = s_near.astype(BF16)
            s_near = jnp.where(causal, s_near * SCALE, MASKED)
        else:
            full, last = s_near[0:lo], s_near[lo:hi]
            raw_i = jnp.concatenate([full, jnp.where(causal, last, 0.0)]).astype(BF16)
            s_near = jnp.concatenate([full * SCALE, jnp.where(causal, last * SCALE, MASKED)])
        raw[0, 0:hi, lo:hi] = raw_i
        head = jnp.where(edge, s_far[0:TILE], MASKED)
        if i < TOK // TILE - 1:
            s_far = jnp.concatenate([head, s_far[TILE:]])
        else:
            s_far = head
        s_far = jnp.where(inside, s_far, MASKED)
        top = jnp.maximum(
            jnp.max(s_near, axis=0, keepdims=True), jnp.max(s_far, axis=0, keepdims=True)
        )
        p_near = jnp.exp(s_near - top)
        p_far = jnp.exp(s_far - top)
        inv = 1.0 / (
            jnp.sum(p_near, axis=0, keepdims=True) + jnp.sum(p_far, axis=0, keepdims=True)
        )
        p_near = (p_near * inv).astype(BF16)
        p_far = (p_far * inv).astype(BF16)
        near[0, 0:hi, lo:hi] = p_near
        far[0, lo:TOK, lo:hi] = p_far
        window[:, lo:hi] = nn(v_t[:, 0:hi], p_near) + nn(vh_t[:, lo:TOK], p_far)
        intra[:, lo:hi] = nn(v_t[:, 0:hi], raw_i)


def mixed_kernel(q, before, window, intra, normed, inverse, mixed_t, mixed):
    lin = intra[...] + nt(flip(before[0]).astype(BF16), q[...])
    inv = lax.rsqrt(jnp.mean(lin * lin, axis=0, keepdims=True) + EPSILON)
    unit = lin * inv
    normed[...] = unit
    inverse[0] = inv
    out = unit + window[...]
    mixed_t[...] = out.astype(BF16)
    mixed[...] = out.T.astype(BF16)


def far_kernel(q, g, kw, vw, far, window, dq, dk, dv, delta, ds):
    g_t = flip(g[...])
    d = jnp.sum(g_t * window[...], axis=0, keepdims=True)
    delta[0] = d
    kh_t = flip(kw[...]).astype(BF16)
    for i in range(TOK // TILE):
        lo, hi = i * TILE, (i + 1) * TILE
        dp = nt(vw[lo:TOK, :], g[lo:hi, :])
        part = (far[0, lo:TOK, lo:hi].astype(F32) * (dp - d[:, lo:hi]) * SCALE).astype(BF16)
        ds[lo:TOK, lo:hi] = part
        dq[:, lo:hi] = nn(kh_t[:, lo:TOK], part)
    for j in range(TOK // TILE):
        lo, hi = j * TILE, (j + 1) * TILE
        dk_j = nn(ds[lo:hi, 0:hi], q[0:hi, :]).astype(BF16)
        dv_j = nn(far[0, lo:hi, 0:hi], g[0:hi, :]).astype(BF16)
        if j == 0:
            dk[0 : hi - BLOCK, :] = dk_j[BLOCK:]
            dv[0 : hi - BLOCK, :] = dv_j[BLOCK:]
        else:
            dk[lo - BLOCK : hi - BLOCK, :] = dk_j
            dv[lo - BLOCK : hi - BLOCK, :] = dv_j


def lin_kernel(q, g, normed, inverse, grad_lin, sums):
    g_t = flip(g[...])
    unit = normed[...]
    inner = jnp.mean(g_t * unit, axis=0, keepdims=True)
    out = inverse[0] * (g_t - unit * inner)
    rows = out.T.astype(BF16)
    grad_lin[...] = rows
    sums[0] = tn(q[...], rows).astype(BF16)


def near_kernel(q, k, v, g, gl, near, raw, before, delta, dq_far, dq, dk, dv, both):
    causal = causal_tile()
    d = delta[0]
    k_t = flip(k[...]).astype(BF16)
    dq_t = dq_far[...] + nt(before[0], gl[...])
    parts = []
    for i in range(TOK // TILE):
        lo, hi = i * TILE, (i + 1) * TILE
        dp = nt(v[0:hi, :], g[lo:hi, :])
        ig = nt(v[0:hi, :], gl[lo:hi, :])
        last = jnp.where(causal, ig[lo:hi], 0.0)
        ig = last if i == 0 else jnp.concatenate([ig[0:lo], last])
        sum_i = near[0, 0:hi, lo:hi].astype(F32) * (dp - d[:, lo:hi]) * SCALE + ig
        sum_i = sum_i.astype(BF16)
        both[0:hi, lo:hi] = sum_i
        parts.append(dq_t[:, lo:hi] + nn(k_t[:, 0:hi], sum_i))
    dq[...] = jnp.concatenate(parts, axis=1).T.astype(BF16)
    for j in range(TOK // TILE):
        lo, hi = j * TILE, (j + 1) * TILE
        dk[lo:hi, :] = nn(both[lo:hi, lo:TOK], q[lo:TOK, :])
        dv[lo:hi, :] = nn(near[0, lo:hi, lo:TOK], g[lo:TOK, :]) + nn(
            raw[0, lo:hi, lo:TOK], gl[lo:TOK, :]
        )


def last_kernel(k, v, later, dk, dv, rk, rv, out_k, out_v):
    state = later[0]
    add_k = dk[...] + nt(v[...], state)
    add_v = dv[...] + nn(k[...], state)
    out_k[0:BLOCK, :] = add_k[0:BLOCK].astype(BF16)
    out_v[0:BLOCK, :] = add_v[0:BLOCK].astype(BF16)
    out_k[BLOCK:TOK, :] = (add_k[BLOCK:] + rk[...].astype(F32)).astype(BF16)
    out_v[BLOCK:TOK, :] = (add_v[BLOCK:] + rv[...].astype(F32)).astype(BF16)


def scan_kernel(backward, x, out):
    total = jnp.zeros(x.shape[1:], F32)
    count = x.shape[0]
    for i in range(count):
        at = count - 1 - i if backward else i
        out[at] = total.astype(BF16)
        total = total + x[at].astype(F32)


def carry_states(local, backward, beside=()):
    count = lax.axis_size("seq")
    pieces = local.reshape(count, -1, DH)
    met = lax.all_to_all(pieces, "seq", 0, 0)
    met, beside = lax.optimization_barrier((met, beside))
    done = pl.pallas_call(
        functools.partial(scan_kernel, backward),
        out_shape=jax.ShapeDtypeStruct(met.shape, BF16),
    )(met)
    return lax.all_to_all(done, "seq", 0, 0).reshape(local.shape), beside


def block_id(t, head):
    hops = jnp.where(t % XS < 2, t % XS, 5 - t % XS)
    x = (head[0] // 2 + XS - hops) % XS
    core = jnp.where(t < XS, head[0] % 2, 1 - head[0] % 2)
    return 2 * x + core


def gathered_specs(rows, width):
    return [pl.BlockSpec((rows, width), lambda t, head: (0, 0))] * (2 * XS)


def weight_specs(part, rest, width):
    return [
        pl.BlockSpec((width // DH, part, DH), lambda t, head: (block_id(t, head), 0, 0)),
        pl.BlockSpec((rest, width), lambda t, head: (0, block_id(t, head))),
    ]


def across(w):
    return jnp.concatenate([w[i] for i in range(w.shape[0])], axis=1)


def each_block(blocks, use):
    for j, block in enumerate(blocks):

        @pl.when(pl.program_id(0) == j)
        def _(block=block):
            use(block[...])


def grad_mixed_kernel(head, *refs):
    blocks, (wa, wb, out, acc) = refs[: 2 * XS], refs[2 * XS :]
    part = wa.shape[1]
    t = pl.program_id(0)

    @pl.when(t == 0)
    def _():
        acc[...] = jnp.zeros_like(acc)

    def add(block):
        acc[:, 0:part] += nt(block, across(wa))
        acc[:, part:] += nt(block, wb[...])

    each_block(blocks, add)

    @pl.when(t == 2 * XS - 1)
    def _():
        out[...] = acc[...].astype(BF16)


def sens_kernel(head, *refs):
    blocks, (mixed_t, out) = refs[: 2 * XS], refs[2 * XS :]

    def put(block):
        out[0] = nn(mixed_t[...], block).astype(BF16)

    each_block(blocks, put)


def mixer_kernel(head, mixed, wa, wb, out):
    part = wa.shape[1]
    out[...] = (nn(mixed[:, 0:part], across(wa)) + nn(mixed[:, part:], wb[...])).astype(BF16)


def fold_kernel(*refs):
    total = refs[0][...].astype(F32)
    for part in refs[1:-1]:
        total = total + part[...].astype(F32)
    refs[-1][0] = total.astype(BF16)


YS, ZS, XS = 4, 8, 4
Y_HOPS = (1, YS - 1, 2)


def shifted(shard, by):
    count = lax.axis_size("seq")
    pairs = [(i, i + by) for i in range(count) if 0 <= i + by < count]
    return lax.ppermute(shard, "seq", pairs)


Z_GROUPS = [[y * ZS + z for z in range(ZS)] for y in range(YS)]
Y_GROUPS = [[y * ZS + z for y in range(YS)] for z in range(ZS)]


def exchange(pieces, axis, groups):
    return lax.all_to_all(pieces, axis, 0, 0, axis_index_groups=groups)


def spread(shard, axis, groups):
    copies = jnp.broadcast_to(shard[None], (len(groups[0]),) + shard.shape)
    return exchange(copies, axis, groups)


def hop_y(shard, by):
    return lax.ppermute(
        shard, "seq", [(y * ZS + z, (y + by) % YS * ZS + z) for y in range(YS) for z in range(ZS)]
    )


def hop_x(shard, by):
    return lax.ppermute(
        shard, "head", [(x * 2 + c, (x + by) % XS * 2 + c) for x in range(XS) for c in range(2)]
    )


def swap_core(shard):
    return lax.ppermute(shard, "head", [(i, i ^ 1) for i in range(2 * XS)])


def shards(queries, keys, values, w_out, grad_y):
    rows, width = queries.shape
    heads = width // DH
    seq = lax.axis_index("seq").reshape(1).astype(jnp.int32)
    head = lax.axis_index("head").reshape(1).astype(jnp.int32)
    tokens_all = rows * lax.axis_size("seq")
    cut = rows // 4
    shape = jax.ShapeDtypeStruct
    col = columns(rows)
    tri = heads_of(rows, rows)
    st = heads_of(DH, DH)
    turned = rows_of(DH, rows)
    line = heads_of(1, rows)
    mm = 2 * rows * rows * width

    wb = lax.all_gather(w_out[cut:], "seq", axis=1, tiled=True)
    grads = [grad_y] + [hop_x(grad_y, by) for by in (1, XS - 1, 2)]
    kh, vh = shifted(keys, 1), shifted(values, 1)

    local = call(
        sums_kernel, heads, [col, col], st, shape((heads, DH, DH), BF16), flops=2 * mm // 4
    )(keys, values)
    before, (kh, vh, grads) = carry_states(local, False, (kh, vh, grads))

    swapped = [swap_core(g) for g in grads]
    before, first, swapped = lax.optimization_barrier((before, w_out[:cut], swapped))
    wa = spread(spread(first, "seq", Z_GROUPS), "seq", Y_GROUPS).reshape(YS * ZS, cut, DH)

    sq = large((heads, rows, rows), BF16)
    flat_t = large((width, rows), F32)
    edge = EDGE
    grads = list(grads) + list(swapped)
    near, far, raw, window, intra = call(
        window_kernel,
        heads,
        [col] * 5,
        [tri, tri, tri, turned, turned],
        [sq, sq, sq, flat_t, flat_t],
        flops=12 * mm // 8,
        size=12 << 20,
        prefetch=1,
    )(seq, queries, keys, values, kh, vh)

    normed, inverse, mixed_t, mixed = call(
        mixed_kernel,
        heads,
        [col, st, turned, turned],
        [turned, line, turned, col],
        [
            flat_t,
            shape((heads, 1, rows), F32),
            large((width, rows), BF16),
            large((rows, width), BF16),
        ],
        flops=mm // 4,
        size=5 << 20,
    )(queries, before, window, intra)

    gathered = gathered_specs(rows, width)
    weights = weight_specs(cut, rows - cut, width)
    out_block = pl.BlockSpec((rows, width), lambda t, head: (0, block_id(t, head)))
    fixed = pl.BlockSpec((rows, width), lambda t, head: (0, 0))
    by_block = functools.partial(call, heads=2 * XS, size=9 << 20, flops=8 * mm, prefetch=1)
    pieces = by_block(
        sens_kernel,
        ins=gathered + [fixed],
        outs=pl.BlockSpec(
            (1, width, width), lambda t, head: (block_id(t, head) // 2, 0, block_id(t, head) % 2)
        ),
        out_shape=large((YS, width, 2 * width), BF16),
    )(head, *grads, mixed_t)
    y = lax.axis_index("seq") // ZS
    own = lax.dynamic_index_in_dim(pieces, y, 0, False)
    sends = [lax.dynamic_index_in_dim(pieces, (y + by) % YS, 0, False) for by in Y_HOPS]
    met = [own] + [hop_y(piece, by) for piece, by in zip(sends, Y_HOPS)]
    own, sends, wa, wb = lax.optimization_barrier((own, sends, wa, wb))

    partial_value = by_block(
        mixer_kernel,
        ins=[fixed] + weights,
        outs=out_block,
        out_shape=large((rows, 2 * XS * width), BF16),
    )(head, mixed, wa, wb)
    mixer_result = lax.psum_scatter(partial_value, "head", scatter_dimension=1, tiled=True)
    grad_mixed = by_block(
        grad_mixed_kernel,
        ins=gathered + weights,
        outs=fixed,
        out_shape=large((rows, width), BF16),
        scratch=[pltpu.VMEM((rows, width), F32)],
    )(head, *grads, wa, wb)

    edge_grad = large((edge, width), BF16)
    dq_far, far_k, far_v, delta = call(
        far_kernel,
        heads,
        [col, col, col, col, tri, turned],
        [turned, columns(edge), columns(edge), line],
        [flat_t, edge_grad, edge_grad, shape((heads, 1, rows), F32)],
        scratch=[pltpu.VMEM((rows, rows), BF16)],
        flops=8 * mm // 8,
        size=8 << 20,
    )(queries, grad_mixed, kh, vh, far, window)
    back_k, back_v = shifted(far_k, -1), shifted(far_v, -1)

    grad_lin, local_back = call(
        lin_kernel,
        heads,
        [col, col, turned, line],
        [col, st],
        [large((rows, width), BF16), shape((heads, DH, DH), BF16)],
        flops=mm // 4,
        size=3 << 20,
    )(queries, grad_mixed, normed, inverse)
    later, _ = carry_states(local_back, True)

    grad_queries, near_k, near_v = call(
        near_kernel,
        heads,
        [col, col, col, col, col, tri, tri, st, line, turned],
        [col, col, col],
        [large((rows, width), BF16), large((rows, width), F32), large((rows, width), F32)],
        scratch=[pltpu.VMEM((rows, rows), BF16)],
        flops=12 * mm // 8,
        size=12 << 20,
    )(queries, keys, values, grad_mixed, grad_lin, near, raw, before, delta, dq_far)

    grad_keys, grad_values = call(
        last_kernel,
        heads,
        [col, col, st, col, col, columns(edge), columns(edge)],
        [col, col],
        [large((rows, width), BF16)] * 2,
        flops=mm // 2,
        size=5 << 20,
    )(keys, values, later, near_k, near_v, back_k, back_v)
    met, _ = lax.optimization_barrier((met, grad_keys))
    parts = call(
        fold_kernel,
        ZS,
        [pl.BlockSpec((width, DH), lambda z: (0, z))] * YS,
        pl.BlockSpec((1, width, DH), lambda z: (z, 0, 0)),
        large((ZS, width, DH), BF16),
        size=5 << 20,
    )(*met)
    total = jnp.sum(exchange(parts, "seq", Z_GROUPS).astype(F32), axis=0)
    projection_sensitivity = total * tokens_all ** (-0.5)

    return (mixer_result, grad_queries, grad_keys, grad_values, projection_sensitivity)


def solution(mesh):
    placed = (
        P("seq", "head"),
        P("seq", "head"),
        P("seq", "head"),
        P("head", "seq"),
        P("seq", "head"),
    )
    return jax.shard_map(
        shards,
        mesh=mesh,
        in_specs=placed,
        out_specs=(
            P("seq", "head"),
            P("seq", "head"),
            P("seq", "head"),
            P("seq", "head"),
            P("head", "seq"),
        ),
        check_vma=False,
    )
```

```python
import functools
import math

import jax
import jax.numpy as jnp
from jax import lax
from jax.experimental import pallas as pl
from jax.experimental.pallas import tpu as pltpu
from jax.sharding import PartitionSpec as P

DH = 128
BLOCK = 64
BAND = 8
TILE = 128
TOK = BAND * BLOCK
EDGE = TOK - BLOCK
SCALE = 1.0 / math.sqrt(DH)
EPSILON = 1e-05
MASKED = -1e30
F32 = jnp.float32
BF16 = jnp.bfloat16


def nn(a, b):
    return lax.dot_general(a, b, (((1,), (0,)), ((), ())), preferred_element_type=F32)


def nt(a, b):
    return lax.dot_general(a, b, (((1,), (1,)), ((), ())), preferred_element_type=F32)


def tn(a, b):
    return lax.dot_general(a, b, (((0,), (0,)), ((), ())), preferred_element_type=F32)


def flip(a):
    return a.astype(F32).T


def call(kernel, heads, ins, outs, out_shape, scratch=(), flops=0, size=0, prefetch=0):
    run = pl.pallas_call(
        kernel,
        grid_spec=pltpu.PrefetchScalarGridSpec(
            num_scalar_prefetch=prefetch,
            grid=(heads,),
            in_specs=ins,
            out_specs=outs,
            scratch_shapes=scratch,
        ),
        out_shape=out_shape,
        compiler_params=pltpu.CompilerParams(
            dimension_semantics=("arbitrary",), vmem_limit_bytes=40 * 1024 * 1024
        ),
        cost_estimate=pl.CostEstimate(flops=flops, bytes_accessed=size, transcendentals=0),
    )
    return lambda *args: run(*args[:prefetch], *(kept(a) for a in args[prefetch:]))


def kept(a):
    return pltpu.with_memory_space_constraint(a, pltpu.HBM)


def large(*args):
    return pltpu.HBM(*args)


def columns(rows, at=0):
    return pl.BlockSpec((rows, DH), lambda h, *_: (at, h))


def heads_of(*dims):
    return pl.BlockSpec((1,) + dims, lambda h, *_: (h,) + (0,) * len(dims))


def rows_of(rows, cols):
    return pl.BlockSpec((rows, cols), lambda h, *_: (h, 0))


def sums_kernel(k, v, out):
    out[0] = tn(k[...], v[...]).astype(BF16)


def causal_tile():
    row = lax.broadcasted_iota(jnp.int32, (TILE, TILE), 0)
    col = lax.broadcasted_iota(jnp.int32, (TILE, TILE), 1)
    return row <= col


def edge_tile():
    row = lax.broadcasted_iota(jnp.int32, (TILE, TILE), 0)
    col = lax.broadcasted_iota(jnp.int32, (TILE, TILE), 1)
    return (row >= BLOCK) & (col < BLOCK)


def window_kernel(place, q, k, v, kw, vw, near, far, raw, window, intra):
    causal, edge = causal_tile(), edge_tile()
    inside = place[0] > 0
    v_t = flip(v[...]).astype(BF16)
    vh_t = flip(vw[...]).astype(BF16)
    for i in range(TOK // TILE):
        lo, hi = i * TILE, (i + 1) * TILE
        q_i = q[lo:hi, :]
        s_near = nt(k[0:hi, :], q_i)
        s_far = nt(kw[lo:TOK, :], q_i) * SCALE
        if i == 0:
            s_near = jnp.where(causal, s_near, 0.0)
            raw_i = s_near.astype(BF16)
            s_near = jnp.where(causal, s_near * SCALE, MASKED)
        else:
            full, last = s_near[0:lo], s_near[lo:hi]
            raw_i = jnp.concatenate([full, jnp.where(causal, last, 0.0)]).astype(BF16)
            s_near = jnp.concatenate([full * SCALE, jnp.where(causal, last * SCALE, MASKED)])
        raw[0, 0:hi, lo:hi] = raw_i
        head = jnp.where(edge, s_far[0:TILE], MASKED)
        if i < TOK // TILE - 1:
            s_far = jnp.concatenate([head, s_far[TILE:]])
        else:
            s_far = head
        s_far = jnp.where(inside, s_far, MASKED)
        top = jnp.maximum(
            jnp.max(s_near, axis=0, keepdims=True), jnp.max(s_far, axis=0, keepdims=True)
        )
        p_near = jnp.exp(s_near - top)
        p_far = jnp.exp(s_far - top)
        inv = 1.0 / (
            jnp.sum(p_near, axis=0, keepdims=True) + jnp.sum(p_far, axis=0, keepdims=True)
        )
        p_near = (p_near * inv).astype(BF16)
        p_far = (p_far * inv).astype(BF16)
        near[0, 0:hi, lo:hi] = p_near
        far[0, lo:TOK, lo:hi] = p_far
        window[:, lo:hi] = nn(v_t[:, 0:hi], p_near) + nn(vh_t[:, lo:TOK], p_far)
        intra[:, lo:hi] = nn(v_t[:, 0:hi], raw_i)


def mixed_kernel(q, before, window, intra, normed, inverse, mixed_t, mixed):
    lin = intra[...] + nt(flip(before[0]).astype(BF16), q[...])
    inv = lax.rsqrt(jnp.mean(lin * lin, axis=0, keepdims=True) + EPSILON)
    unit = lin * inv
    normed[...] = unit
    inverse[0] = inv
    out = unit + window[...]
    mixed_t[...] = out.astype(BF16)
    mixed[...] = out.T.astype(BF16)


def far_kernel(q, g, kw, vw, far, window, dq, dk, dv, delta, ds):
    g_t = flip(g[...])
    d = jnp.sum(g_t * window[...], axis=0, keepdims=True)
    delta[0] = d
    kh_t = flip(kw[...]).astype(BF16)
    for i in range(TOK // TILE):
        lo, hi = i * TILE, (i + 1) * TILE
        dp = nt(vw[lo:TOK, :], g[lo:hi, :])
        part = (far[0, lo:TOK, lo:hi].astype(F32) * (dp - d[:, lo:hi]) * SCALE).astype(BF16)
        ds[lo:TOK, lo:hi] = part
        dq[:, lo:hi] = nn(kh_t[:, lo:TOK], part)
    for j in range(TOK // TILE):
        lo, hi = j * TILE, (j + 1) * TILE
        dk_j = nn(ds[lo:hi, 0:hi], q[0:hi, :]).astype(BF16)
        dv_j = nn(far[0, lo:hi, 0:hi], g[0:hi, :]).astype(BF16)
        if j == 0:
            dk[0 : hi - BLOCK, :] = dk_j[BLOCK:]
            dv[0 : hi - BLOCK, :] = dv_j[BLOCK:]
        else:
            dk[lo - BLOCK : hi - BLOCK, :] = dk_j
            dv[lo - BLOCK : hi - BLOCK, :] = dv_j


def lin_kernel(q, g, normed, inverse, grad_lin, sums):
    g_t = flip(g[...])
    unit = normed[...]
    inner = jnp.mean(g_t * unit, axis=0, keepdims=True)
    out = inverse[0] * (g_t - unit * inner)
    rows = out.T.astype(BF16)
    grad_lin[...] = rows
    sums[0] = tn(q[...], rows).astype(BF16)


def near_kernel(q, k, v, g, gl, near, raw, before, delta, dq_far, dq, dk, dv, both):
    causal = causal_tile()
    d = delta[0]
    k_t = flip(k[...]).astype(BF16)
    dq_t = dq_far[...] + nt(before[0], gl[...])
    parts = []
    for i in range(TOK // TILE):
        lo, hi = i * TILE, (i + 1) * TILE
        dp = nt(v[0:hi, :], g[lo:hi, :])
        ig = nt(v[0:hi, :], gl[lo:hi, :])
        last = jnp.where(causal, ig[lo:hi], 0.0)
        ig = last if i == 0 else jnp.concatenate([ig[0:lo], last])
        sum_i = near[0, 0:hi, lo:hi].astype(F32) * (dp - d[:, lo:hi]) * SCALE + ig
        sum_i = sum_i.astype(BF16)
        both[0:hi, lo:hi] = sum_i
        parts.append(dq_t[:, lo:hi] + nn(k_t[:, 0:hi], sum_i))
    dq[...] = jnp.concatenate(parts, axis=1).T.astype(BF16)
    for j in range(TOK // TILE):
        lo, hi = j * TILE, (j + 1) * TILE
        dk[lo:hi, :] = nn(both[lo:hi, lo:TOK], q[lo:TOK, :])
        dv[lo:hi, :] = nn(near[0, lo:hi, lo:TOK], g[lo:TOK, :]) + nn(
            raw[0, lo:hi, lo:TOK], gl[lo:TOK, :]
        )


def last_kernel(k, v, later, dk, dv, rk, rv, out_k, out_v):
    state = later[0]
    add_k = dk[...] + nt(v[...], state)
    add_v = dv[...] + nn(k[...], state)
    out_k[0:BLOCK, :] = add_k[0:BLOCK].astype(BF16)
    out_v[0:BLOCK, :] = add_v[0:BLOCK].astype(BF16)
    out_k[BLOCK:TOK, :] = (add_k[BLOCK:] + rk[...].astype(F32)).astype(BF16)
    out_v[BLOCK:TOK, :] = (add_v[BLOCK:] + rv[...].astype(F32)).astype(BF16)


def scan_kernel(backward, x, out):
    total = jnp.zeros(x.shape[1:], F32)
    count = x.shape[0]
    for i in range(count):
        at = count - 1 - i if backward else i
        out[at] = total.astype(BF16)
        total = total + x[at].astype(F32)


def carry_states(local, backward, beside=()):
    count = lax.axis_size("seq")
    pieces = local.reshape(count, -1, DH)
    met = lax.all_to_all(pieces, "seq", 0, 0)
    met, beside = lax.optimization_barrier((met, beside))
    done = pl.pallas_call(
        functools.partial(scan_kernel, backward),
        out_shape=jax.ShapeDtypeStruct(met.shape, BF16),
    )(met)
    return lax.all_to_all(done, "seq", 0, 0).reshape(local.shape), beside


def block_id(t, head):
    hops = jnp.where(t % XS < 2, t % XS, 5 - t % XS)
    x = (head[0] // 2 + XS - hops) % XS
    core = jnp.where(t < XS, head[0] % 2, 1 - head[0] % 2)
    return 2 * x + core


def gathered_specs(rows, width):
    return [pl.BlockSpec((rows, width), lambda t, *_: (0, 0))] * (2 * XS)


def each_block(blocks, use):
    for j, block in enumerate(blocks):

        @pl.when(pl.program_id(0) == j)
        def _(block=block):
            use(block[...])


def project_kernel(head, y, *refs):
    blocks, rest = refs[: 2 * XS], refs[2 * XS :]
    mixed, near_w, far_w = rest[0], rest[1 : 1 + YS], rest[1 + YS]
    partial_value, out, acc, w = rest[2 + YS :]
    t = pl.program_id(0)
    part = near_w[0].shape[1]
    shards_in = far_w.shape[0]
    block = block_id(t, head)
    slot = (y[0] + YS - block // 2) % YS

    @pl.when(t == 0)
    def _():
        acc[...] = jnp.zeros_like(acc)

    for r, source in enumerate(near_w):

        @pl.when(slot == r)
        def _(source=source):
            for i in range(shards_in):
                w[0:part, i * DH : (i + 1) * DH] = source[block % 2 * shards_in + i]

    for i in range(shards_in):
        w[part:, i * DH : (i + 1) * DH] = far_w[i, 0]
    partial_value[...] = nn(mixed[...], w[...]).astype(BF16)

    def add(block):
        acc[...] += nt(block, w[...])

    each_block(blocks, add)

    @pl.when(t == 2 * XS - 1)
    def _():
        out[...] = acc[...].astype(BF16)


def sens_kernel(head, y, *refs):
    blocks, (mixed_t, *outs) = refs[: 2 * XS], refs[2 * XS :]
    block = block_id(pl.program_id(0), head)
    slot = (block // 2 + YS - y[0]) % YS
    width = mixed_t.shape[0]
    at = pl.ds(pl.multiple_of(block % 2 * width, width), width)

    def put(block):
        part = nn(mixed_t[...], block).astype(BF16)
        for r, out in enumerate(outs):

            @pl.when(slot == r)
            def _(out=out):
                out[:, at] = part

    each_block(blocks, put)


def fold_kernel(*refs):
    total = refs[0][...].astype(F32)
    for part in refs[1:-1]:
        total = total + part[...].astype(F32)
    refs[-1][0] = total.astype(BF16)


YS, ZS, XS = 4, 8, 4
Y_HOPS = (1, YS - 1, 2)


def shifted(shard, by):
    count = lax.axis_size("seq")
    pairs = [(i, i + by) for i in range(count) if 0 <= i + by < count]
    return lax.ppermute(shard, "seq", pairs)


Z_GROUPS = [[y * ZS + z for z in range(ZS)] for y in range(YS)]
Y_GROUPS = [[y * ZS + z for y in range(YS)] for z in range(ZS)]


def exchange(pieces, axis, groups):
    return lax.all_to_all(pieces, axis, 0, 0, axis_index_groups=groups)


def spread(shard, axis, groups):
    copies = jnp.broadcast_to(shard[None], (len(groups[0]),) + shard.shape)
    return exchange(copies, axis, groups)


def hop_y(shard, by):
    return lax.ppermute(
        shard, "seq", [(y * ZS + z, (y + by) % YS * ZS + z) for y in range(YS) for z in range(ZS)]
    )


def hop_x(shard, by):
    return lax.ppermute(
        shard, "head", [(x * 2 + c, (x + by) % XS * 2 + c) for x in range(XS) for c in range(2)]
    )


def swap_core(shard):
    return lax.ppermute(shard, "head", [(i, i ^ 1) for i in range(2 * XS)])


def shards(queries, keys, values, w_out, grad_y):
    rows, width = queries.shape
    heads = width // DH
    seq = lax.axis_index("seq").reshape(1).astype(jnp.int32)
    head = lax.axis_index("head").reshape(1).astype(jnp.int32)
    tokens_all = rows * lax.axis_size("seq")
    shape = jax.ShapeDtypeStruct
    col = columns(rows)
    tri = heads_of(rows, rows)
    st = heads_of(DH, DH)
    turned = rows_of(DH, rows)
    line = heads_of(1, rows)
    mm = 2 * rows * rows * width

    half = rows // 2
    far_w = w_out[half:]
    far_w = jnp.stack([far_w] + [hop_y(far_w, by) for by in range(1, YS)])
    far_w = lax.all_gather(far_w, "seq", axis_index_groups=Z_GROUPS)
    local = call(
        sums_kernel, heads, [col, col], st, shape((heads, DH, DH), BF16), flops=2 * mm // 4
    )(keys, values)
    local, grad, k_out, v_out = lax.optimization_barrier((local, grad_y, keys, values))
    hopped = [hop_x(grad, by) for by in (1, XS - 1, 2)]
    kh, vh = shifted(k_out, 1), shifted(v_out, 1)
    before, (kh, vh, hopped) = carry_states(local, False, (kh, vh, hopped))
    grads = [grad_y] + list(hopped)
    swapped = [swap_core(g) for g in grads]

    near_w = spread(w_out[:half], "seq", Z_GROUPS)
    near_w = [near_w] + [hop_y(near_w, by) for by in range(1, YS)]

    sq = large((heads, rows, rows), BF16)
    flat_t = large((width, rows), F32)
    edge = EDGE
    near, far, raw, window, intra = call(
        window_kernel,
        heads,
        [col] * 5,
        [tri, tri, tri, turned, turned],
        [sq, sq, sq, flat_t, flat_t],
        flops=12 * mm // 8,
        size=12 << 20,
        prefetch=1,
    )(seq, queries, keys, values, kh, vh)

    before, window = lax.optimization_barrier((before, window))
    grads = grads + swapped
    normed, inverse, mixed_t, mixed = call(
        mixed_kernel,
        heads,
        [col, st, turned, turned],
        [turned, line, turned, col],
        [
            flat_t,
            shape((heads, 1, rows), F32),
            large((width, rows), BF16),
            large((rows, width), BF16),
        ],
        flops=mm // 4,
        size=5 << 20,
    )(queries, before, window, intra)

    gathered = gathered_specs(rows, width)
    fixed = pl.BlockSpec((rows, width), lambda t, *_: (0, 0))
    by_block = functools.partial(call, heads=2 * XS, size=9 << 20, flops=8 * mm)
    y = (lax.axis_index("seq") // ZS).reshape(1).astype(jnp.int32)
    pieces = by_block(
        sens_kernel,
        ins=gathered + [fixed],
        outs=[pl.BlockSpec((width, 2 * width), lambda t, *_: (0, 0))] * YS,
        out_shape=[large((width, 2 * width), BF16)] * YS,
        prefetch=2,
    )(head, y, *grads, mixed_t)
    met = [pieces[0]] + [hop_y(pieces[by], by) for by in Y_HOPS]
    pieces, far_w = lax.optimization_barrier((pieces, far_w))

    partial_value, grad_mixed = by_block(
        project_kernel,
        ins=gathered
        + [fixed]
        + [pl.BlockSpec((ZS, half, DH), lambda t, *_: (0, 0, 0))] * YS
        + [
            pl.BlockSpec(
                (ZS // 2, 1, half, DH),
                lambda t, head, y: (
                    block_id(t, head) % 2,
                    (y[0] + YS - block_id(t, head) // 2) % YS,
                    0,
                    0,
                ),
            )
        ],
        outs=[pl.BlockSpec((rows, width), lambda t, head, y: (0, block_id(t, head))), fixed],
        out_shape=[large((rows, 2 * XS * width), BF16), large((rows, width), BF16)],
        scratch=[pltpu.VMEM((rows, width), F32), pltpu.VMEM((rows, width), BF16)],
        prefetch=2,
    )(head, y, *grads, mixed, *near_w, far_w)
    mixer_result = lax.psum_scatter(partial_value, "head", scatter_dimension=1, tiled=True)

    edge_grad = large((edge, width), BF16)
    dq_far, far_k, far_v, delta = call(
        far_kernel,
        heads,
        [col, col, col, col, tri, turned],
        [turned, columns(edge), columns(edge), line],
        [flat_t, edge_grad, edge_grad, shape((heads, 1, rows), F32)],
        scratch=[pltpu.VMEM((rows, rows), BF16)],
        flops=8 * mm // 8,
        size=8 << 20,
    )(queries, grad_mixed, kh, vh, far, window)
    back_k, back_v = shifted(far_k, -1), shifted(far_v, -1)

    grad_lin, local_back = call(
        lin_kernel,
        heads,
        [col, col, turned, line],
        [col, st],
        [large((rows, width), BF16), shape((heads, DH, DH), BF16)],
        flops=mm // 4,
        size=3 << 20,
    )(queries, grad_mixed, normed, inverse)
    later, _ = carry_states(local_back, True)

    grad_queries, near_k, near_v = call(
        near_kernel,
        heads,
        [col, col, col, col, col, tri, tri, st, line, turned],
        [col, col, col],
        [large((rows, width), BF16), large((rows, width), F32), large((rows, width), F32)],
        scratch=[pltpu.VMEM((rows, rows), BF16)],
        flops=12 * mm // 8,
        size=12 << 20,
    )(queries, keys, values, grad_mixed, grad_lin, near, raw, before, delta, dq_far)

    grad_keys, grad_values = call(
        last_kernel,
        heads,
        [col, col, st, col, col, columns(edge), columns(edge)],
        [col, col],
        [large((rows, width), BF16)] * 2,
        flops=mm // 2,
        size=5 << 20,
    )(keys, values, later, near_k, near_v, back_k, back_v)
    met, _ = lax.optimization_barrier((met, grad_keys))
    parts = call(
        fold_kernel,
        ZS,
        [pl.BlockSpec((width, DH), lambda z: (0, z))] * YS,
        pl.BlockSpec((1, width, DH), lambda z: (z, 0, 0)),
        large((ZS, width, DH), BF16),
        size=5 << 20,
    )(*met)
    total = jnp.sum(exchange(parts, "seq", Z_GROUPS).astype(F32), axis=0)
    projection_sensitivity = total * tokens_all ** (-0.5)

    return (mixer_result, grad_queries, grad_keys, grad_values, projection_sensitivity)


def solution(mesh):
    placed = (
        P("seq", "head"),
        P("seq", "head"),
        P("seq", "head"),
        P("head", "seq"),
        P("seq", "head"),
    )
    return jax.shard_map(
        shards,
        mesh=mesh,
        in_specs=placed,
        out_specs=(
            P("seq", "head"),
            P("seq", "head"),
            P("seq", "head"),
            P("seq", "head"),
            P("head", "seq"),
        ),
        check_vma=False,
    )
```

```python
import functools
import math

import jax
import jax.numpy as jnp
from jax import lax
from jax.experimental import pallas as pl
from jax.experimental.pallas import tpu as pltpu
from jax.sharding import PartitionSpec as P

DH = 128
BLOCK = 64
BAND = 8
TILE = 128
TOK = BAND * BLOCK
EDGE = TOK - BLOCK
SCALE = 1.0 / math.sqrt(DH)
EPSILON = 1e-05
MASKED = -1e30
F32 = jnp.float32
BF16 = jnp.bfloat16


def nn(a, b):
    return lax.dot_general(a, b, (((1,), (0,)), ((), ())), preferred_element_type=F32)


def nt(a, b):
    return lax.dot_general(a, b, (((1,), (1,)), ((), ())), preferred_element_type=F32)


def tn(a, b):
    return lax.dot_general(a, b, (((0,), (0,)), ((), ())), preferred_element_type=F32)


def flip(a):
    return a.astype(F32).T


def call(kernel, heads, ins, outs, out_shape, scratch=(), flops=0, size=0, prefetch=0):
    run = pl.pallas_call(
        kernel,
        grid_spec=pltpu.PrefetchScalarGridSpec(
            num_scalar_prefetch=prefetch,
            grid=heads if isinstance(heads, tuple) else (heads,),
            in_specs=ins,
            out_specs=outs,
            scratch_shapes=scratch,
        ),
        out_shape=out_shape,
        compiler_params=pltpu.CompilerParams(
            vmem_limit_bytes=40 * 1024 * 1024
        ),
        cost_estimate=pl.CostEstimate(flops=0, bytes_accessed=0, transcendentals=0),
    )
    return lambda *args: run(*args[:prefetch], *(kept(a) for a in args[prefetch:]))


def kept(a):
    return pltpu.with_memory_space_constraint(a, pltpu.HBM)


def large(*args):
    return pltpu.HBM(*args)


def columns(rows, at=0):
    return pl.BlockSpec((rows, DH), lambda h, *_: (at, h))


def heads_of(*dims):
    return pl.BlockSpec((1,) + dims, lambda h, *_: (h,) + (0,) * len(dims))


def rows_of(rows, cols):
    return pl.BlockSpec((rows, cols), lambda h, *_: (h, 0))


def sums_kernel(k, v, out):
    out[0] = tn(k[...], v[...]).astype(BF16)


def causal_tile():
    row = lax.broadcasted_iota(jnp.int32, (TILE, TILE), 0)
    col = lax.broadcasted_iota(jnp.int32, (TILE, TILE), 1)
    return row <= col


def edge_tile():
    row = lax.broadcasted_iota(jnp.int32, (TILE, TILE), 0)
    col = lax.broadcasted_iota(jnp.int32, (TILE, TILE), 1)
    return (row >= BLOCK) & (col < BLOCK)


def window_kernel(place, q, k, v, kw, vw, near, far, raw, window, intra):
    causal, edge = causal_tile(), edge_tile()
    inside = place[0] > 0
    v_t = flip(v[...]).astype(BF16)
    vh_t = flip(vw[...]).astype(BF16)
    for i in range(TOK // TILE):
        lo, hi = i * TILE, (i + 1) * TILE
        q_i = q[lo:hi, :]
        s_near = nt(k[0:hi, :], q_i)
        s_far = nt(kw[lo:TOK, :], q_i) * SCALE
        if i == 0:
            s_near = jnp.where(causal, s_near, 0.0)
            raw_i = s_near.astype(BF16)
            s_near = jnp.where(causal, s_near * SCALE, MASKED)
        else:
            full, last = s_near[0:lo], s_near[lo:hi]
            raw_i = jnp.concatenate([full, jnp.where(causal, last, 0.0)]).astype(BF16)
            s_near = jnp.concatenate([full * SCALE, jnp.where(causal, last * SCALE, MASKED)])
        raw[0, 0:hi, lo:hi] = raw_i
        head = jnp.where(edge, s_far[0:TILE], MASKED)
        if i < TOK // TILE - 1:
            s_far = jnp.concatenate([head, s_far[TILE:]])
        else:
            s_far = head
        s_far = jnp.where(inside, s_far, MASKED)
        top = jnp.maximum(
            jnp.max(s_near, axis=0, keepdims=True), jnp.max(s_far, axis=0, keepdims=True)
        )
        p_near = jnp.exp(s_near - top)
        p_far = jnp.exp(s_far - top)
        inv = 1.0 / (
            jnp.sum(p_near, axis=0, keepdims=True) + jnp.sum(p_far, axis=0, keepdims=True)
        )
        p_near = (p_near * inv).astype(BF16)
        p_far = (p_far * inv).astype(BF16)
        near[0, 0:hi, lo:hi] = p_near
        far[0, lo:TOK, lo:hi] = p_far
        window[:, lo:hi] = nn(v_t[:, 0:hi], p_near) + nn(vh_t[:, lo:TOK], p_far)
        intra[:, lo:hi] = nn(v_t[:, 0:hi], raw_i)


def mixed_kernel(q, before, window, intra, normed, inverse, mixed_t, mixed):
    lin = intra[...] + nt(flip(before[0]).astype(BF16), q[...])
    inv = lax.rsqrt(jnp.mean(lin * lin, axis=0, keepdims=True) + EPSILON)
    unit = lin * inv
    normed[...] = unit
    inverse[0] = inv
    out = unit + window[...]
    mixed_t[...] = out.astype(BF16)
    mixed[...] = out.T.astype(BF16)


def far_kernel(q, g, kw, vw, far, window, dq, dk, dv, delta, ds):
    g_t = flip(g[...])
    d = jnp.sum(g_t * window[...], axis=0, keepdims=True)
    delta[0] = d
    kh_t = flip(kw[...]).astype(BF16)
    for i in range(TOK // TILE):
        lo, hi = i * TILE, (i + 1) * TILE
        dp = nt(vw[lo:TOK, :], g[lo:hi, :])
        part = (far[0, lo:TOK, lo:hi].astype(F32) * (dp - d[:, lo:hi]) * SCALE).astype(BF16)
        ds[lo:TOK, lo:hi] = part
        dq[:, lo:hi] = nn(kh_t[:, lo:TOK], part)
    for j in range(TOK // TILE):
        lo, hi = j * TILE, (j + 1) * TILE
        dk_j = nn(ds[lo:hi, 0:hi], q[0:hi, :]).astype(BF16)
        dv_j = nn(far[0, lo:hi, 0:hi], g[0:hi, :]).astype(BF16)
        if j == 0:
            dk[0 : hi - BLOCK, :] = dk_j[BLOCK:]
            dv[0 : hi - BLOCK, :] = dv_j[BLOCK:]
        else:
            dk[lo - BLOCK : hi - BLOCK, :] = dk_j
            dv[lo - BLOCK : hi - BLOCK, :] = dv_j


def lin_kernel(q, g, normed, inverse, grad_lin, sums):
    g_t = flip(g[...])
    unit = normed[...]
    inner = jnp.mean(g_t * unit, axis=0, keepdims=True)
    out = inverse[0] * (g_t - unit * inner)
    rows = out.T.astype(BF16)
    grad_lin[...] = rows
    sums[0] = tn(q[...], rows).astype(BF16)


def near_kernel(q, k, v, g, gl, near, raw, before, delta, dq_far, dq, dk, dv, both):
    causal = causal_tile()
    d = delta[0]
    k_t = flip(k[...]).astype(BF16)
    dq_t = dq_far[...] + nt(before[0], gl[...])
    parts = []
    for i in range(TOK // TILE):
        lo, hi = i * TILE, (i + 1) * TILE
        dp = nt(v[0:hi, :], g[lo:hi, :])
        ig = nt(v[0:hi, :], gl[lo:hi, :])
        last = jnp.where(causal, ig[lo:hi], 0.0)
        ig = last if i == 0 else jnp.concatenate([ig[0:lo], last])
        sum_i = near[0, 0:hi, lo:hi].astype(F32) * (dp - d[:, lo:hi]) * SCALE + ig
        sum_i = sum_i.astype(BF16)
        both[0:hi, lo:hi] = sum_i
        parts.append(dq_t[:, lo:hi] + nn(k_t[:, 0:hi], sum_i))
    dq[...] = jnp.concatenate(parts, axis=1).T.astype(BF16)
    for j in range(TOK // TILE):
        lo, hi = j * TILE, (j + 1) * TILE
        dk[lo:hi, :] = nn(both[lo:hi, lo:TOK], q[lo:TOK, :])
        dv[lo:hi, :] = nn(near[0, lo:hi, lo:TOK], g[lo:TOK, :]) + nn(
            raw[0, lo:hi, lo:TOK], gl[lo:TOK, :]
        )


def last_kernel(k, v, later, dk, dv, rk, rv, out_k, out_v):
    state = later[0]
    add_k = dk[...] + nt(v[...], state)
    add_v = dv[...] + nn(k[...], state)
    out_k[0:BLOCK, :] = add_k[0:BLOCK].astype(BF16)
    out_v[0:BLOCK, :] = add_v[0:BLOCK].astype(BF16)
    out_k[BLOCK:TOK, :] = (add_k[BLOCK:] + rk[...].astype(F32)).astype(BF16)
    out_v[BLOCK:TOK, :] = (add_v[BLOCK:] + rv[...].astype(F32)).astype(BF16)


def scan_kernel(backward, x, out):
    total = jnp.zeros(x.shape[1:], F32)
    count = x.shape[0]
    for i in range(count):
        at = count - 1 - i if backward else i
        out[at] = total.astype(BF16)
        total = total + x[at].astype(F32)


def carry_states(local, backward):
    count = lax.axis_size("seq")
    pieces = local.reshape(count, -1, DH)
    met = lax.all_to_all(pieces, "seq", 0, 0)
    done = pl.pallas_call(
        functools.partial(scan_kernel, backward),
        out_shape=jax.ShapeDtypeStruct(met.shape, BF16),
    )(met)
    return lax.all_to_all(done, "seq", 0, 0).reshape(local.shape)


def project_kernel(y, g, mixed, *refs):
    sources, (partial_value, out, acc, w) = refs[:YS], refs[YS:]
    block = pl.program_id(0)
    count = sources[0].shape[0] // 2
    slot = (y[0] + YS - block // 2) % YS

    @pl.when(block == 0)
    def _():
        acc[...] = jnp.zeros_like(acc)

    for r, source in enumerate(sources):

        @pl.when(slot == r)
        def _(source=source):
            for i in range(count):
                w[:, i * DH : (i + 1) * DH] = source[block % 2 * count + i]

    partial_value[...] = nn(mixed[...], w[...]).astype(BF16)
    acc[...] += nt(g[...], w[...])

    @pl.when(block == 2 * XS - 1)
    def _():
        out[...] = acc[...].astype(BF16)


def sens_kernel(place, g, *refs):
    sources, outs, acc = refs[:YS], refs[YS:-1], refs[-1]
    half, turn = pl.program_id(0), pl.program_id(1)

    @pl.when(turn == 0)
    def _():
        acc[...] = jnp.zeros_like(acc)

    for r, source in enumerate(sources):

        @pl.when(turn == r)
        def _(source=source):
            acc[...] += nn(source[...], g[...])

    @pl.when(turn == YS - 1)
    def _():
        count = ZS // 2
        for i in range(count):
            slot = (half * count + i + ZS - place[1]) % ZS
            part = acc[:, i * DH : (i + 1) * DH].astype(BF16)
            for r, out in enumerate(outs):

                @pl.when(slot == r)
                def _(out=out, part=part):
                    out[...] = part


YS, ZS, XS = 4, 8, 4
Y_HOPS = (1, YS - 1, 2)


def shifted(shard, by):
    count = lax.axis_size("seq")
    pairs = [(i, i + by) for i in range(count) if 0 <= i + by < count]
    return lax.ppermute(shard, "seq", pairs)


Z_GROUPS = [[y * ZS + z for z in range(ZS)] for y in range(YS)]
Y_GROUPS = [[y * ZS + z for y in range(YS)] for z in range(ZS)]


def exchange(pieces, axis, groups):
    return lax.all_to_all(pieces, axis, 0, 0, axis_index_groups=groups)


def spread(shard, axis, groups):
    copies = jnp.broadcast_to(shard[None], (len(groups[0]),) + shard.shape)
    return exchange(copies, axis, groups)


def hop_y(shard, by):
    return lax.ppermute(
        shard, "seq", [(y * ZS + z, (y + by) % YS * ZS + z) for y in range(YS) for z in range(ZS)]
    )


def hop_z(shard, by):
    return lax.ppermute(
        shard, "seq", [(y * ZS + z, y * ZS + (z + by) % ZS) for y in range(YS) for z in range(ZS)]
    )


def turn_xy(shard):
    pairs = [
        ((y * ZS + z) * 2 * XS + 2 * x + c, (x * ZS + z) * 2 * XS + 2 * y + c)
        for y in range(YS)
        for z in range(ZS)
        for x in range(XS)
        for c in range(2)
    ]
    return lax.ppermute(shard, ("seq", "head"), pairs)


def shards(queries, keys, values, w_out, grad_y):
    rows, width = queries.shape
    heads = width // DH
    seq = lax.axis_index("seq").reshape(1).astype(jnp.int32)
    tokens_all = rows * lax.axis_size("seq")
    shape = jax.ShapeDtypeStruct
    col = columns(rows)
    tri = heads_of(rows, rows)
    st = heads_of(DH, DH)
    turned = rows_of(DH, rows)
    line = heads_of(1, rows)
    mm = 2 * rows * rows * width

    place = jnp.concatenate([seq // ZS, seq % ZS])

    grad_full = lax.all_gather(grad_y, "head", axis=1, tiled=True)
    turned_grad = turn_xy(grad_y)
    w_row = spread(w_out, "seq", Z_GROUPS)
    local = call(
        sums_kernel, heads, [col, col], st, shape((heads, DH, DH), BF16), flops=2 * mm // 4
    )(keys, values)
    local, w_row, turned_grad = lax.optimization_barrier((local, w_row, turned_grad))
    grad_wide = lax.all_gather(turned_grad, "head", axis=1, tiled=True)
    w_rows = [w_row] + [hop_y(w_row, by) for by in range(1, YS)]
    kh, vh = shifted(keys, 1), shifted(values, 1)
    before = carry_states(local, False)

    sq = large((heads, rows, rows), BF16)
    flat_t = large((width, rows), F32)
    edge = EDGE
    near, far, raw, window, intra = call(
        window_kernel,
        heads,
        [col] * 5,
        [tri, tri, tri, turned, turned],
        [sq, sq, sq, flat_t, flat_t],
        flops=12 * mm // 8,
        size=12 << 20,
        prefetch=1,
    )(seq, queries, keys, values, kh, vh)

    before, window = lax.optimization_barrier((before, window))
    normed, inverse, mixed_t, mixed = call(
        mixed_kernel,
        heads,
        [col, st, turned, turned],
        [turned, line, turned, col],
        [
            flat_t,
            shape((heads, 1, rows), F32),
            large((width, rows), BF16),
            large((rows, width), BF16),
        ],
        flops=mm // 4,
        size=5 << 20,
    )(queries, before, window, intra)

    w_rows, before = lax.optimization_barrier((w_rows, before))
    across_y = [mixed_t] + [hop_y(mixed_t, by) for by in range(1, YS)]
    fixed = pl.BlockSpec((rows, width), lambda *_: (0, 0))
    by_block = pl.BlockSpec((rows, width), lambda b, *_: (0, b))
    partial_value, grad_mixed = call(
        project_kernel,
        2 * XS,
        [by_block, fixed] + [pl.BlockSpec((ZS, rows, DH), lambda *_: (0, 0, 0))] * YS,
        [by_block, fixed],
        [large((rows, 2 * XS * width), BF16), large((rows, width), BF16)],
        scratch=[pltpu.VMEM((rows, width), F32), pltpu.VMEM((rows, width), BF16)],
        prefetch=1,
    )(place, grad_full, mixed, *w_rows)
    mixer_result = lax.psum_scatter(partial_value, "head", scatter_dimension=1, tiled=True)

    grad_lin, local_back = call(
        lin_kernel,
        heads,
        [col, col, turned, line],
        [col, st],
        [large((rows, width), BF16), shape((heads, DH, DH), BF16)],
        flops=mm // 4,
        size=3 << 20,
    )(queries, grad_mixed, normed, inverse)
    local_back, g_far = lax.optimization_barrier((local_back, grad_mixed))
    edge_grad = large((edge, width), BF16)
    dq_far, far_k, far_v, delta = call(
        far_kernel,
        heads,
        [col, col, col, col, tri, turned],
        [turned, columns(edge), columns(edge), line],
        [flat_t, edge_grad, edge_grad, shape((heads, 1, rows), F32)],
        scratch=[pltpu.VMEM((rows, rows), BF16)],
        flops=8 * mm // 8,
        size=8 << 20,
    )(queries, g_far, kh, vh, far, window)
    back_k, back_v = shifted(far_k, -1), shifted(far_v, -1)

    later = carry_states(local_back, True)

    across_y, local_back = lax.optimization_barrier((across_y, local_back))
    parts = call(
        sens_kernel,
        (2, YS),
        [
            pl.BlockSpec(
                (rows, width), lambda c, by, place: (0, (place[0] + YS - by) % YS * 2 + c)
            )
        ]
        + [fixed] * YS,
        [pl.BlockSpec((width, DH), lambda *_: (0, 0))] * ZS,
        [large((width, DH), BF16)] * ZS,
        scratch=[pltpu.VMEM((width, rows), F32)],
        prefetch=1,
    )(place, grad_wide, *across_y)
    total = parts[0].astype(F32)
    for by in range(1, ZS):
        total = total + hop_z(parts[by], by).astype(F32)
    projection_sensitivity = total * tokens_all ** (-0.5)

    grad_queries, near_k, near_v = call(
        near_kernel,
        heads,
        [col, col, col, col, col, tri, tri, st, line, turned],
        [col, col, col],
        [large((rows, width), BF16), large((rows, width), F32), large((rows, width), F32)],
        scratch=[pltpu.VMEM((rows, rows), BF16)],
        flops=12 * mm // 8,
        size=12 << 20,
    )(queries, keys, values, grad_mixed, grad_lin, near, raw, before, delta, dq_far)

    grad_keys, grad_values = call(
        last_kernel,
        heads,
        [col, col, st, col, col, columns(edge), columns(edge)],
        [col, col],
        [large((rows, width), BF16)] * 2,
        flops=mm // 2,
        size=5 << 20,
    )(keys, values, later, near_k, near_v, back_k, back_v)
    return (mixer_result, grad_queries, grad_keys, grad_values, projection_sensitivity)


def solution(mesh):
    placed = (
        P("seq", "head"),
        P("seq", "head"),
        P("seq", "head"),
        P("head", "seq"),
        P("seq", "head"),
    )
    return jax.shard_map(
        shards,
        mesh=mesh,
        in_specs=placed,
        out_specs=(
            P("seq", "head"),
            P("seq", "head"),
            P("seq", "head"),
            P("seq", "head"),
            P("head", "seq"),
        ),
        check_vma=False,
    )
```

```python
import functools
import math

import jax
import jax.numpy as jnp
from jax import lax
from jax.experimental import pallas as pl
from jax.experimental.pallas import tpu as pltpu
from jax.sharding import PartitionSpec as P

DH = 128
BLOCK = 64
BAND = 8
TILE = 128
TOK = BAND * BLOCK
EDGE = TOK - BLOCK
SCALE = 1.0 / math.sqrt(DH)
EPSILON = 1e-05
MASKED = -1e30
F32 = jnp.float32
BF16 = jnp.bfloat16


def nn(a, b):
    return lax.dot_general(a, b, (((1,), (0,)), ((), ())), preferred_element_type=F32)


def nt(a, b):
    return lax.dot_general(a, b, (((1,), (1,)), ((), ())), preferred_element_type=F32)


def tn(a, b):
    return lax.dot_general(a, b, (((0,), (0,)), ((), ())), preferred_element_type=F32)


def flip(a):
    return a.astype(F32).T


def call(kernel, heads, ins, outs, out_shape, scratch=(), flops=0, size=0, prefetch=0):
    run = pl.pallas_call(
        kernel,
        grid_spec=pltpu.PrefetchScalarGridSpec(
            num_scalar_prefetch=prefetch,
            grid=heads if isinstance(heads, tuple) else (heads,),
            in_specs=ins,
            out_specs=outs,
            scratch_shapes=scratch,
        ),
        out_shape=out_shape,
        compiler_params=pltpu.CompilerParams(
            vmem_limit_bytes=40 * 1024 * 1024
        ),
        cost_estimate=pl.CostEstimate(flops=0, bytes_accessed=0, transcendentals=0),
    )
    return lambda *args: run(*args[:prefetch], *(kept(a) for a in args[prefetch:]))


def kept(a):
    return pltpu.with_memory_space_constraint(a, pltpu.HBM)


def large(*args):
    return pltpu.HBM(*args)


def columns(rows, at=0):
    return pl.BlockSpec((rows, DH), lambda h, *_: (at, h))


def heads_of(*dims):
    return pl.BlockSpec((1,) + dims, lambda h, *_: (h,) + (0,) * len(dims))


def rows_of(rows, cols):
    return pl.BlockSpec((rows, cols), lambda h, *_: (h, 0))


def sums_kernel(k, v, out):
    out[0] = tn(k[...], v[...]).astype(BF16)


def causal_tile():
    row = lax.broadcasted_iota(jnp.int32, (TILE, TILE), 0)
    col = lax.broadcasted_iota(jnp.int32, (TILE, TILE), 1)
    return row <= col


def edge_tile():
    row = lax.broadcasted_iota(jnp.int32, (TILE, TILE), 0)
    col = lax.broadcasted_iota(jnp.int32, (TILE, TILE), 1)
    return (row >= BLOCK) & (col < BLOCK)


def window_kernel(place, q, k, v, kw, vw, near, far, raw, window, intra):
    causal, edge = causal_tile(), edge_tile()
    inside = place[0] > 0
    v_t = flip(v[...]).astype(BF16)
    vh_t = flip(vw[...]).astype(BF16)
    for i in range(TOK // TILE):
        lo, hi = i * TILE, (i + 1) * TILE
        q_i = q[lo:hi, :]
        s_near = nt(k[0:hi, :], q_i)
        s_far = nt(kw[lo:TOK, :], q_i) * SCALE
        if i == 0:
            s_near = jnp.where(causal, s_near, 0.0)
            raw_i = s_near.astype(BF16)
            s_near = jnp.where(causal, s_near * SCALE, MASKED)
        else:
            full, last = s_near[0:lo], s_near[lo:hi]
            raw_i = jnp.concatenate([full, jnp.where(causal, last, 0.0)]).astype(BF16)
            s_near = jnp.concatenate([full * SCALE, jnp.where(causal, last * SCALE, MASKED)])
        raw[0, 0:hi, lo:hi] = raw_i
        head = jnp.where(edge, s_far[0:TILE], MASKED)
        if i < TOK // TILE - 1:
            s_far = jnp.concatenate([head, s_far[TILE:]])
        else:
            s_far = head
        s_far = jnp.where(inside, s_far, MASKED)
        top = jnp.maximum(
            jnp.max(s_near, axis=0, keepdims=True), jnp.max(s_far, axis=0, keepdims=True)
        )
        p_near = jnp.exp(s_near - top)
        p_far = jnp.exp(s_far - top)
        inv = 1.0 / (
            jnp.sum(p_near, axis=0, keepdims=True) + jnp.sum(p_far, axis=0, keepdims=True)
        )
        p_near = (p_near * inv).astype(BF16)
        p_far = (p_far * inv).astype(BF16)
        near[0, 0:hi, lo:hi] = p_near
        far[0, lo:TOK, lo:hi] = p_far
        window[:, lo:hi] = nn(v_t[:, 0:hi], p_near) + nn(vh_t[:, lo:TOK], p_far)
        intra[:, lo:hi] = nn(v_t[:, 0:hi], raw_i)


def mixed_kernel(q, before, window, intra, normed, inverse, mixed_t, mixed):
    lin = intra[...] + nt(flip(before[0]).astype(BF16), q[...])
    inv = lax.rsqrt(jnp.mean(lin * lin, axis=0, keepdims=True) + EPSILON)
    unit = lin * inv
    normed[...] = unit
    inverse[0] = inv
    out = unit + window[...]
    mixed_t[...] = out.astype(BF16)
    mixed[...] = out.T.astype(BF16)


def far_kernel(q, g, kw, vw, far, window, dq, dk, dv, delta, ds):
    g_t = flip(g[...])
    d = jnp.sum(g_t * window[...], axis=0, keepdims=True)
    delta[0] = d
    kh_t = flip(kw[...]).astype(BF16)
    for i in range(TOK // TILE):
        lo, hi = i * TILE, (i + 1) * TILE
        dp = nt(vw[lo:TOK, :], g[lo:hi, :])
        part = (far[0, lo:TOK, lo:hi].astype(F32) * (dp - d[:, lo:hi]) * SCALE).astype(BF16)
        ds[lo:TOK, lo:hi] = part
        dq[:, lo:hi] = nn(kh_t[:, lo:TOK], part)
    for j in range(TOK // TILE):
        lo, hi = j * TILE, (j + 1) * TILE
        dk_j = nn(ds[lo:hi, 0:hi], q[0:hi, :]).astype(BF16)
        dv_j = nn(far[0, lo:hi, 0:hi], g[0:hi, :]).astype(BF16)
        if j == 0:
            dk[0 : hi - BLOCK, :] = dk_j[BLOCK:]
            dv[0 : hi - BLOCK, :] = dv_j[BLOCK:]
        else:
            dk[lo - BLOCK : hi - BLOCK, :] = dk_j
            dv[lo - BLOCK : hi - BLOCK, :] = dv_j


def lin_kernel(q, g, normed, inverse, grad_lin, sums):
    g_t = flip(g[...])
    unit = normed[...]
    inner = jnp.mean(g_t * unit, axis=0, keepdims=True)
    out = inverse[0] * (g_t - unit * inner)
    rows = out.T.astype(BF16)
    grad_lin[...] = rows
    sums[0] = tn(q[...], rows).astype(BF16)


def near_kernel(q, k, v, g, gl, near, raw, before, delta, dq_far, dq, dk, dv, both):
    causal = causal_tile()
    d = delta[0]
    k_t = flip(k[...]).astype(BF16)
    dq_t = dq_far[...] + nt(before[0], gl[...])
    parts = []
    for i in range(TOK // TILE):
        lo, hi = i * TILE, (i + 1) * TILE
        dp = nt(v[0:hi, :], g[lo:hi, :])
        ig = nt(v[0:hi, :], gl[lo:hi, :])
        last = jnp.where(causal, ig[lo:hi], 0.0)
        ig = last if i == 0 else jnp.concatenate([ig[0:lo], last])
        sum_i = near[0, 0:hi, lo:hi].astype(F32) * (dp - d[:, lo:hi]) * SCALE + ig
        sum_i = sum_i.astype(BF16)
        both[0:hi, lo:hi] = sum_i
        parts.append(dq_t[:, lo:hi] + nn(k_t[:, 0:hi], sum_i))
    dq[...] = jnp.concatenate(parts, axis=1).T.astype(BF16)
    for j in range(TOK // TILE):
        lo, hi = j * TILE, (j + 1) * TILE
        dk[lo:hi, :] = nn(both[lo:hi, lo:TOK], q[lo:TOK, :])
        dv[lo:hi, :] = nn(near[0, lo:hi, lo:TOK], g[lo:TOK, :]) + nn(
            raw[0, lo:hi, lo:TOK], gl[lo:TOK, :]
        )


def last_kernel(k, v, later, dk, dv, rk, rv, out_k, out_v):
    state = later[0]
    add_k = dk[...] + nt(v[...], state)
    add_v = dv[...] + nn(k[...], state)
    out_k[0:BLOCK, :] = add_k[0:BLOCK].astype(BF16)
    out_v[0:BLOCK, :] = add_v[0:BLOCK].astype(BF16)
    out_k[BLOCK:TOK, :] = (add_k[BLOCK:] + rk[...].astype(F32)).astype(BF16)
    out_v[BLOCK:TOK, :] = (add_v[BLOCK:] + rv[...].astype(F32)).astype(BF16)


def scan_kernel(backward, x, out):
    total = jnp.zeros(x.shape[1:], F32)
    count = x.shape[0]
    for i in range(count):
        at = count - 1 - i if backward else i
        out[at] = total.astype(BF16)
        total = total + x[at].astype(F32)


def carry_states(local, backward, beside=(), between=()):
    count = lax.axis_size("seq")
    pieces = local.reshape(count, -1, DH)
    met = lax.all_to_all(pieces, "seq", 0, 0)
    met, between = lax.optimization_barrier((met, between))
    done = pl.pallas_call(
        functools.partial(scan_kernel, backward),
        out_shape=jax.ShapeDtypeStruct(met.shape, BF16),
    )(met)
    done, beside = lax.optimization_barrier((done, beside))
    return lax.all_to_all(done, "seq", 0, 0).reshape(local.shape), beside, between


def block_id(t, head):
    x = (head[0] // 2 + XS - t % XS) % XS
    core = jnp.where(t < XS, head[0] % 2, 1 - head[0] % 2)
    return 2 * x + core


def project_kernel(head, mixed, w, *refs):
    blocks, (partial_value, out, acc) = refs[:-3], refs[-3:]
    t = pl.program_id(0)

    @pl.when(t == 0)
    def _():
        acc[...] = jnp.zeros_like(acc)

    partial_value[...] = nn(mixed[...], w[...]).astype(BF16)
    for j, block in enumerate(blocks):

        @pl.when(t == j)
        def _(block=block):
            acc[...] += nt(block[...], w[...])

    @pl.when(t == len(blocks) - 1)
    def _():
        out[...] = acc[...].astype(BF16)


def sens_kernel(place, mine, other, *refs):
    sources, outs, acc = refs[:YS], refs[YS:-1], refs[-1]
    side, turn = pl.program_id(0), pl.program_id(1)
    half = jnp.where(side == 0, place[2], 1 - place[2])

    @pl.when(turn == 0)
    def _():
        acc[...] = jnp.zeros_like(acc)

    for r, source in enumerate(sources):

        @pl.when((turn == r) & (side == 0))
        def _(source=source):
            acc[...] += nn(source[...], mine[0])

        @pl.when((turn == r) & (side == 1))
        def _(source=source):
            acc[...] += nn(source[...], other[0])

    @pl.when(turn == YS - 1)
    def _():
        count = ZS // 2
        for i in range(count):
            slot = (half * count + i + ZS - place[1]) % ZS
            part = acc[:, i * DH : (i + 1) * DH].astype(BF16)
            for r, out in enumerate(outs):

                @pl.when(slot == r)
                def _(out=out, part=part):
                    out[...] = part


YS, ZS, XS = 4, 8, 4
Y_HOPS = (1, YS - 1, 2)


def shifted(shard, by):
    count = lax.axis_size("seq")
    pairs = [(i, i + by) for i in range(count) if 0 <= i + by < count]
    return lax.ppermute(shard, "seq", pairs)


Z_GROUPS = [[y * ZS + z for z in range(ZS)] for y in range(YS)]
Y_GROUPS = [[y * ZS + z for y in range(YS)] for z in range(ZS)]


def exchange(pieces, axis, groups):
    return lax.all_to_all(pieces, axis, 0, 0, axis_index_groups=groups)


def spread(shard, axis, groups):
    copies = jnp.broadcast_to(shard[None], (len(groups[0]),) + shard.shape)
    return exchange(copies, axis, groups)


def hop_y(shard, by):
    return lax.ppermute(
        shard, "seq", [(y * ZS + z, (y + by) % YS * ZS + z) for y in range(YS) for z in range(ZS)]
    )


X_GROUPS = [[2 * x + c for x in range(XS)] for c in range(2)]


def hop_x(shard, by):
    return lax.ppermute(
        shard, "head", [(x * 2 + c, (x + by) % XS * 2 + c) for x in range(XS) for c in range(2)]
    )


def swap_core(shard):
    return lax.ppermute(shard, "head", [(i, i ^ 1) for i in range(2 * XS)])


def hop_z(shard, by):
    return lax.ppermute(
        shard, "seq", [(y * ZS + z, y * ZS + (z + by) % ZS) for y in range(YS) for z in range(ZS)]
    )


def turn_xy(shard):
    pairs = [
        ((y * ZS + z) * 2 * XS + 2 * x + c, (x * ZS + z) * 2 * XS + 2 * y + c)
        for y in range(YS)
        for z in range(ZS)
        for x in range(XS)
        for c in range(2)
    ]
    return lax.ppermute(shard, ("seq", "head"), pairs)


def shards(queries, keys, values, w_out, grad_y):
    rows, width = queries.shape
    heads = width // DH
    seq = lax.axis_index("seq").reshape(1).astype(jnp.int32)
    tokens_all = rows * lax.axis_size("seq")
    shape = jax.ShapeDtypeStruct
    col = columns(rows)
    tri = heads_of(rows, rows)
    st = heads_of(DH, DH)
    turned = rows_of(DH, rows)
    line = heads_of(1, rows)
    mm = 2 * rows * rows * width

    head = lax.axis_index("head").reshape(1).astype(jnp.int32)
    place = jnp.concatenate([seq // ZS, seq % ZS, head % 2])

    full_w = lax.all_gather(w_out, "seq", axis=1, tiled=True)
    hopped = [hop_x(grad_y, by) for by in range(1, XS)]
    local = call(
        sums_kernel, heads, [col, col], st, shape((heads, DH, DH), BF16), flops=2 * mm // 4
    )(keys, values)
    before, _, sent = carry_states(local, False, (), (keys, values, grad_y))
    kh, vh, turned_grad = shifted(sent[0], 1), shifted(sent[1], 1), turn_xy(sent[2])
    before, kh, vh, hopped, turned_grad = lax.optimization_barrier(
        (before, kh, vh, hopped, turned_grad)
    )
    grads = [grad_y] + hopped
    grads = grads + [swap_core(g) for g in grads]

    sq = large((heads, rows, rows), BF16)
    flat_t = large((width, rows), F32)
    edge = EDGE
    near, far, raw, window, intra = call(
        window_kernel,
        heads,
        [col] * 5,
        [tri, tri, tri, turned, turned],
        [sq, sq, sq, flat_t, flat_t],
        flops=12 * mm // 8,
        size=12 << 20,
        prefetch=1,
    )(seq, queries, keys, values, kh, vh)

    before, window = lax.optimization_barrier((before, window))
    normed, inverse, mixed_t, mixed = call(
        mixed_kernel,
        heads,
        [col, st, turned, turned],
        [turned, line, turned, col],
        [
            flat_t,
            shape((heads, 1, rows), F32),
            large((width, rows), BF16),
            large((rows, width), BF16),
        ],
        flops=mm // 4,
        size=5 << 20,
    )(queries, before, window, intra)

    turned_grad, mixed_t = lax.optimization_barrier((turned_grad, mixed_t))
    mine = spread(turned_grad, "head", X_GROUPS)
    across_y = [mixed_t] + [hop_y(mixed_t, by) for by in range(1, YS)]
    mine, across_y, full_w = lax.optimization_barrier((mine, across_y, full_w))
    other = swap_core(mine)
    fixed = pl.BlockSpec((rows, width), lambda *_: (0, 0))
    by_block = pl.BlockSpec((rows, width), lambda t, head: (0, block_id(t, head)))
    partial_value, grad_mixed = call(
        project_kernel,
        2 * XS,
        [fixed, by_block] + [fixed] * (2 * XS),
        [by_block, fixed],
        [large((rows, 2 * XS * width), BF16), large((rows, width), BF16)],
        scratch=[pltpu.VMEM((rows, width), F32)],
        prefetch=1,
    )(head, mixed, full_w, *grads)
    mixer_result = lax.psum_scatter(partial_value, "head", scatter_dimension=1, tiled=True)

    grad_lin, local_back = call(
        lin_kernel,
        heads,
        [col, col, turned, line],
        [col, st],
        [large((rows, width), BF16), shape((heads, DH, DH), BF16)],
        flops=mm // 4,
        size=3 << 20,
    )(queries, grad_mixed, normed, inverse)
    local_back, g_far = lax.optimization_barrier((local_back, grad_mixed))
    edge_grad = large((edge, width), BF16)
    dq_far, far_k, far_v, delta = call(
        far_kernel,
        heads,
        [col, col, col, col, tri, turned],
        [turned, columns(edge), columns(edge), line],
        [flat_t, edge_grad, edge_grad, shape((heads, 1, rows), F32)],
        scratch=[pltpu.VMEM((rows, rows), BF16)],
        flops=8 * mm // 8,
        size=8 << 20,
    )(queries, g_far, kh, vh, far, window)
    back_k, back_v = shifted(far_k, -1), shifted(far_v, -1)

    later, grad_lin, _ = carry_states(local_back, True, grad_lin)

    across_y, mine, other, local_back = lax.optimization_barrier(
        (across_y, mine, other, local_back)
    )
    parts = call(
        sens_kernel,
        (2, YS),
        [
            pl.BlockSpec(
                (1, rows, width),
                lambda s, by, place: (
                    jnp.where(s == 0, (place[0] + YS - by) % YS, (place[0] + 1) % YS), 0, 0
                ),
            ),
            pl.BlockSpec(
                (1, rows, width),
                lambda s, by, place: (
                    jnp.where(s == 1, (place[0] + YS - by) % YS, place[0] % YS), 0, 0
                ),
            ),
        ]
        + [fixed] * YS,
        [pl.BlockSpec((width, DH), lambda *_: (0, 0))] * ZS,
        [large((width, DH), BF16)] * ZS,
        scratch=[pltpu.VMEM((width, rows), F32)],
        prefetch=1,
    )(place, mine, other, *across_y)
    total = parts[0].astype(F32)
    for by in range(1, ZS):
        total = total + hop_z(parts[by], by).astype(F32)
    projection_sensitivity = total * tokens_all ** (-0.5)

    grad_queries, near_k, near_v = call(
        near_kernel,
        heads,
        [col, col, col, col, col, tri, tri, st, line, turned],
        [col, col, col],
        [large((rows, width), BF16), large((rows, width), F32), large((rows, width), F32)],
        scratch=[pltpu.VMEM((rows, rows), BF16)],
        flops=12 * mm // 8,
        size=12 << 20,
    )(queries, keys, values, grad_mixed, grad_lin, near, raw, before, delta, dq_far)

    grad_keys, grad_values = call(
        last_kernel,
        heads,
        [col, col, st, col, col, columns(edge), columns(edge)],
        [col, col],
        [large((rows, width), BF16)] * 2,
        flops=mm // 2,
        size=5 << 20,
    )(keys, values, later, near_k, near_v, back_k, back_v)
    return (mixer_result, grad_queries, grad_keys, grad_values, projection_sensitivity)


def solution(mesh):
    placed = (
        P("seq", "head"),
        P("seq", "head"),
        P("seq", "head"),
        P("head", "seq"),
        P("seq", "head"),
    )
    return jax.shard_map(
        shards,
        mesh=mesh,
        in_specs=placed,
        out_specs=(
            P("seq", "head"),
            P("seq", "head"),
            P("seq", "head"),
            P("seq", "head"),
            P("head", "seq"),
        ),
        check_vma=False,
    )
```

```python
import functools
import math

import jax
import jax.numpy as jnp
from jax import lax
from jax.experimental import pallas as pl
from jax.experimental.pallas import tpu as pltpu
from jax.sharding import PartitionSpec as P

DH = 128
BLOCK = 64
BAND = 8
TILE = 128
TOK = BAND * BLOCK
EDGE = TOK - BLOCK
SCALE = 1.0 / math.sqrt(DH)
EPSILON = 1e-05
MASKED = -1e30
F32 = jnp.float32
BF16 = jnp.bfloat16


def nn(a, b):
    return lax.dot_general(a, b, (((1,), (0,)), ((), ())), preferred_element_type=F32)


def nt(a, b):
    return lax.dot_general(a, b, (((1,), (1,)), ((), ())), preferred_element_type=F32)


def tn(a, b):
    return lax.dot_general(a, b, (((0,), (0,)), ((), ())), preferred_element_type=F32)


def flip(a):
    return a.astype(F32).T


def call(kernel, heads, ins, outs, out_shape, scratch=(), flops=0, size=0, prefetch=0):
    run = pl.pallas_call(
        kernel,
        grid_spec=pltpu.PrefetchScalarGridSpec(
            num_scalar_prefetch=prefetch,
            grid=heads if isinstance(heads, tuple) else (heads,),
            in_specs=ins,
            out_specs=outs,
            scratch_shapes=scratch,
        ),
        out_shape=out_shape,
        compiler_params=pltpu.CompilerParams(
            vmem_limit_bytes=40 * 1024 * 1024
        ),
        cost_estimate=pl.CostEstimate(flops=0, bytes_accessed=0, transcendentals=0),
    )
    return lambda *args: run(*args[:prefetch], *(kept(a) for a in args[prefetch:]))


def kept(a):
    return pltpu.with_memory_space_constraint(a, pltpu.HBM)


def large(*args):
    return pltpu.HBM(*args)


def columns(rows, at=0):
    return pl.BlockSpec((rows, DH), lambda h, *_: (at, h))


def heads_of(*dims):
    return pl.BlockSpec((1,) + dims, lambda h, *_: (h,) + (0,) * len(dims))


def rows_of(rows, cols):
    return pl.BlockSpec((rows, cols), lambda h, *_: (h, 0))


def sums_kernel(k, v, out):
    out[0] = tn(k[...], v[...]).astype(BF16)


def causal_tile():
    row = lax.broadcasted_iota(jnp.int32, (TILE, TILE), 0)
    col = lax.broadcasted_iota(jnp.int32, (TILE, TILE), 1)
    return row <= col


def edge_tile():
    row = lax.broadcasted_iota(jnp.int32, (TILE, TILE), 0)
    col = lax.broadcasted_iota(jnp.int32, (TILE, TILE), 1)
    return (row >= BLOCK) & (col < BLOCK)


def window_kernel(place, q, k, v, kw, vw, near, far, raw, window, intra):
    causal, edge = causal_tile(), edge_tile()
    inside = place[0] > 0
    v_t = flip(v[...]).astype(BF16)
    vh_t = flip(vw[...]).astype(BF16)
    for i in range(TOK // TILE):
        lo, hi = i * TILE, (i + 1) * TILE
        q_i = q[lo:hi, :]
        s_near = nt(k[0:hi, :], q_i)
        s_far = nt(kw[lo:TOK, :], q_i) * SCALE
        if i == 0:
            s_near = jnp.where(causal, s_near, 0.0)
            raw_i = s_near.astype(BF16)
            s_near = jnp.where(causal, s_near * SCALE, MASKED)
        else:
            full, last = s_near[0:lo], s_near[lo:hi]
            raw_i = jnp.concatenate([full, jnp.where(causal, last, 0.0)]).astype(BF16)
            s_near = jnp.concatenate([full * SCALE, jnp.where(causal, last * SCALE, MASKED)])
        raw[0, 0:hi, lo:hi] = raw_i
        head = jnp.where(edge, s_far[0:TILE], MASKED)
        if i < TOK // TILE - 1:
            s_far = jnp.concatenate([head, s_far[TILE:]])
        else:
            s_far = head
        s_far = jnp.where(inside, s_far, MASKED)
        top = jnp.maximum(
            jnp.max(s_near, axis=0, keepdims=True), jnp.max(s_far, axis=0, keepdims=True)
        )
        p_near = jnp.exp(s_near - top)
        p_far = jnp.exp(s_far - top)
        inv = 1.0 / (
            jnp.sum(p_near, axis=0, keepdims=True) + jnp.sum(p_far, axis=0, keepdims=True)
        )
        p_near = (p_near * inv).astype(BF16)
        p_far = (p_far * inv).astype(BF16)
        near[0, 0:hi, lo:hi] = p_near
        far[0, lo:TOK, lo:hi] = p_far
        window[:, lo:hi] = nn(v_t[:, 0:hi], p_near) + nn(vh_t[:, lo:TOK], p_far)
        intra[:, lo:hi] = nn(v_t[:, 0:hi], raw_i)


def mixed_kernel(q, before, window, intra, normed, inverse, mixed_t, mixed):
    lin = intra[...] + nt(flip(before[0]).astype(BF16), q[...])
    inv = lax.rsqrt(jnp.mean(lin * lin, axis=0, keepdims=True) + EPSILON)
    unit = lin * inv
    normed[...] = unit
    inverse[0] = inv
    out = unit + window[...]
    mixed_t[...] = out.astype(BF16)
    mixed[...] = out.T.astype(BF16)


def far_kernel(q, g, kw, vw, far, window, dq, dk, dv, delta, ds):
    g_t = flip(g[...])
    d = jnp.sum(g_t * window[...], axis=0, keepdims=True)
    delta[0] = d
    kh_t = flip(kw[...]).astype(BF16)
    for i in range(TOK // TILE):
        lo, hi = i * TILE, (i + 1) * TILE
        dp = nt(vw[lo:TOK, :], g[lo:hi, :])
        part = (far[0, lo:TOK, lo:hi].astype(F32) * (dp - d[:, lo:hi]) * SCALE).astype(BF16)
        ds[lo:TOK, lo:hi] = part
        dq[:, lo:hi] = nn(kh_t[:, lo:TOK], part)
    for j in range(TOK // TILE):
        lo, hi = j * TILE, (j + 1) * TILE
        dk_j = nn(ds[lo:hi, 0:hi], q[0:hi, :]).astype(BF16)
        dv_j = nn(far[0, lo:hi, 0:hi], g[0:hi, :]).astype(BF16)
        if j == 0:
            dk[0 : hi - BLOCK, :] = dk_j[BLOCK:]
            dv[0 : hi - BLOCK, :] = dv_j[BLOCK:]
        else:
            dk[lo - BLOCK : hi - BLOCK, :] = dk_j
            dv[lo - BLOCK : hi - BLOCK, :] = dv_j


def lin_kernel(q, g, normed, inverse, grad_lin, sums):
    g_t = flip(g[...])
    unit = normed[...]
    inner = jnp.mean(g_t * unit, axis=0, keepdims=True)
    out = inverse[0] * (g_t - unit * inner)
    rows = out.T.astype(BF16)
    grad_lin[...] = rows
    sums[0] = tn(q[...], rows).astype(BF16)


def near_kernel(q, k, v, g, gl, near, raw, before, delta, dq_far, dq, dk, dv, both):
    causal = causal_tile()
    d = delta[0]
    k_t = flip(k[...]).astype(BF16)
    dq_t = dq_far[...] + nt(before[0], gl[...])
    parts = []
    for i in range(TOK // TILE):
        lo, hi = i * TILE, (i + 1) * TILE
        dp = nt(v[0:hi, :], g[lo:hi, :])
        ig = nt(v[0:hi, :], gl[lo:hi, :])
        last = jnp.where(causal, ig[lo:hi], 0.0)
        ig = last if i == 0 else jnp.concatenate([ig[0:lo], last])
        sum_i = near[0, 0:hi, lo:hi].astype(F32) * (dp - d[:, lo:hi]) * SCALE + ig
        sum_i = sum_i.astype(BF16)
        both[0:hi, lo:hi] = sum_i
        parts.append(dq_t[:, lo:hi] + nn(k_t[:, 0:hi], sum_i))
    dq[...] = jnp.concatenate(parts, axis=1).T.astype(BF16)
    for j in range(TOK // TILE):
        lo, hi = j * TILE, (j + 1) * TILE
        dk[lo:hi, :] = nn(both[lo:hi, lo:TOK], q[lo:TOK, :])
        dv[lo:hi, :] = nn(near[0, lo:hi, lo:TOK], g[lo:TOK, :]) + nn(
            raw[0, lo:hi, lo:TOK], gl[lo:TOK, :]
        )


def last_kernel(k, v, later, dk, dv, rk, rv, out_k, out_v):
    state = later[0]
    add_k = dk[...] + nt(v[...], state)
    add_v = dv[...] + nn(k[...], state)
    out_k[0:BLOCK, :] = add_k[0:BLOCK].astype(BF16)
    out_v[0:BLOCK, :] = add_v[0:BLOCK].astype(BF16)
    out_k[BLOCK:TOK, :] = (add_k[BLOCK:] + rk[...].astype(F32)).astype(BF16)
    out_v[BLOCK:TOK, :] = (add_v[BLOCK:] + rv[...].astype(F32)).astype(BF16)


def scan_kernel(backward, x, out):
    total = jnp.zeros(x.shape[1:], F32)
    count = x.shape[0]
    for i in range(count):
        at = count - 1 - i if backward else i
        out[at] = total.astype(BF16)
        total = total + x[at].astype(F32)


def carry_states(local, backward, beside=(), between=()):
    count = lax.axis_size("seq")
    pieces = local.reshape(count, -1, DH)
    met = lax.all_to_all(pieces, "seq", 0, 0)
    met, between = lax.optimization_barrier((met, between))
    done = pl.pallas_call(
        functools.partial(scan_kernel, backward),
        out_shape=jax.ShapeDtypeStruct(met.shape, BF16),
    )(met)
    done, beside = lax.optimization_barrier((done, beside))
    return lax.all_to_all(done, "seq", 0, 0).reshape(local.shape), beside, between


def block_id(t, head):
    x = (head[0] // 2 + XS - t % XS) % XS
    core = jnp.where(t < XS, head[0] % 2, 1 - head[0] % 2)
    return 2 * x + core


def project_kernel(head, mixed, w, *refs):
    blocks, (partial_value, out, acc) = refs[:-3], refs[-3:]
    t = pl.program_id(0)

    @pl.when(t == 0)
    def _():
        acc[...] = jnp.zeros_like(acc)

    partial_value[...] = nn(mixed[...], w[...]).astype(BF16)
    for j, block in enumerate(blocks):

        @pl.when(t == j)
        def _(block=block):
            acc[...] += nt(block[...], w[...])

    @pl.when(t == len(blocks) - 1)
    def _():
        out[...] = acc[...].astype(BF16)


def sens_kernel(place, mine, other, *refs):
    sources, outs, acc = refs[:YS], refs[YS:-1], refs[-1]
    side, turn = pl.program_id(0), pl.program_id(1)
    half = jnp.where(side == 0, place[2], 1 - place[2])

    @pl.when(turn == 0)
    def _():
        acc[...] = jnp.zeros_like(acc)

    for r, source in enumerate(sources):

        @pl.when((turn == r) & (side == 0))
        def _(source=source):
            acc[...] += nn(source[...], mine[0])

        @pl.when((turn == r) & (side == 1))
        def _(source=source):
            acc[...] += nn(source[...], other[0])

    @pl.when(turn == YS - 1)
    def _():
        count = ZS // 2
        for i in range(count):
            slot = (half * count + i + ZS - place[1]) % ZS
            part = acc[:, i * DH : (i + 1) * DH].astype(BF16)
            for r, out in enumerate(outs):

                @pl.when(slot == r)
                def _(out=out, part=part):
                    out[...] = part


YS, ZS, XS = 4, 8, 4
Y_HOPS = (1, YS - 1, 2)


def shifted(shard, by):
    count = lax.axis_size("seq")
    pairs = [(i, i + by) for i in range(count) if 0 <= i + by < count]
    return lax.ppermute(shard, "seq", pairs)


Z_GROUPS = [[y * ZS + z for z in range(ZS)] for y in range(YS)]
Y_GROUPS = [[y * ZS + z for y in range(YS)] for z in range(ZS)]


def exchange(pieces, axis, groups):
    return lax.all_to_all(pieces, axis, 0, 0, axis_index_groups=groups)


def spread(shard, axis, groups):
    copies = jnp.broadcast_to(shard[None], (len(groups[0]),) + shard.shape)
    return exchange(copies, axis, groups)


def hop_y(shard, by):
    return lax.ppermute(
        shard, "seq", [(y * ZS + z, (y + by) % YS * ZS + z) for y in range(YS) for z in range(ZS)]
    )


X_GROUPS = [[2 * x + c for x in range(XS)] for c in range(2)]


def hop_x(shard, by):
    return lax.ppermute(
        shard, "head", [(x * 2 + c, (x + by) % XS * 2 + c) for x in range(XS) for c in range(2)]
    )


def swap_core(shard):
    return lax.ppermute(shard, "head", [(i, i ^ 1) for i in range(2 * XS)])


def hop_z(shard, by):
    return lax.ppermute(
        shard, "seq", [(y * ZS + z, y * ZS + (z + by) % ZS) for y in range(YS) for z in range(ZS)]
    )


def turn_xy(shard):
    pairs = [
        ((y * ZS + z) * 2 * XS + 2 * x + c, (x * ZS + z) * 2 * XS + 2 * y + c)
        for y in range(YS)
        for z in range(ZS)
        for x in range(XS)
        for c in range(2)
    ]
    return lax.ppermute(shard, ("seq", "head"), pairs)


def shards(queries, keys, values, w_out, grad_y):
    rows, width = queries.shape
    heads = width // DH
    seq = lax.axis_index("seq").reshape(1).astype(jnp.int32)
    tokens_all = rows * lax.axis_size("seq")
    shape = jax.ShapeDtypeStruct
    col = columns(rows)
    tri = heads_of(rows, rows)
    st = heads_of(DH, DH)
    turned = rows_of(DH, rows)
    line = heads_of(1, rows)
    mm = 2 * rows * rows * width

    head = lax.axis_index("head").reshape(1).astype(jnp.int32)
    place = jnp.concatenate([seq // ZS, seq % ZS, head % 2])

    full_w = lax.all_gather(w_out, "seq", axis=1, tiled=True)
    hopped = [hop_x(grad_y, by) for by in range(1, XS)]
    local = call(
        sums_kernel, heads, [col, col], st, shape((heads, DH, DH), BF16), flops=2 * mm // 4
    )(keys, values)
    local, k_out, v_out = lax.optimization_barrier((local, keys, values))
    kh, vh = shifted(k_out, 1), shifted(v_out, 1)
    before, grad_out, _ = carry_states(local, False, grad_y)
    turned_grad = turn_xy(grad_out)

    sq = large((heads, rows, rows), BF16)
    flat_t = large((width, rows), F32)
    edge = EDGE
    near, far, raw, window, intra = call(
        window_kernel,
        heads,
        [col] * 5,
        [tri, tri, tri, turned, turned],
        [sq, sq, sq, flat_t, flat_t],
        flops=12 * mm // 8,
        size=12 << 20,
        prefetch=1,
    )(seq, queries, keys, values, kh, vh)

    before, window = lax.optimization_barrier((before, window))
    normed, inverse, mixed_t, mixed = call(
        mixed_kernel,
        heads,
        [col, st, turned, turned],
        [turned, line, turned, col],
        [
            flat_t,
            shape((heads, 1, rows), F32),
            large((width, rows), BF16),
            large((rows, width), BF16),
        ],
        flops=mm // 4,
        size=5 << 20,
    )(queries, before, window, intra)

    turned_grad, hopped, mixed_t = lax.optimization_barrier((turned_grad, hopped, mixed_t))
    mine = spread(turned_grad, "head", X_GROUPS)
    across_y = [mixed_t] + [hop_y(mixed_t, by) for by in range(1, YS)]
    mine, across_y = lax.optimization_barrier((mine, across_y))
    grads = [grad_y] + hopped
    grads = grads + [swap_core(g) for g in grads]
    other = swap_core(mine)
    fixed = pl.BlockSpec((rows, width), lambda *_: (0, 0))
    parts = call(
        sens_kernel,
        (2, YS),
        [
            pl.BlockSpec(
                (1, rows, width),
                lambda s, by, place: (
                    jnp.where(s == 0, (place[0] + YS - by) % YS, (place[0] + 1) % YS), 0, 0
                ),
            ),
            pl.BlockSpec(
                (1, rows, width),
                lambda s, by, place: (
                    jnp.where(s == 1, (place[0] + YS - by) % YS, place[0] % YS), 0, 0
                ),
            ),
        ]
        + [fixed] * YS,
        [pl.BlockSpec((width, DH), lambda *_: (0, 0))] * ZS,
        [large((width, DH), BF16)] * ZS,
        scratch=[pltpu.VMEM((width, rows), F32)],
        prefetch=1,
    )(place, mine, other, *across_y)
    parts, full_w = lax.optimization_barrier((parts, full_w))
    by_block = pl.BlockSpec((rows, width), lambda t, head: (0, block_id(t, head)))
    partial_value, grad_mixed = call(
        project_kernel,
        2 * XS,
        [fixed, by_block] + [fixed] * (2 * XS),
        [by_block, fixed],
        [large((rows, 2 * XS * width), BF16), large((rows, width), BF16)],
        scratch=[pltpu.VMEM((rows, width), F32)],
        prefetch=1,
    )(head, mixed, full_w, *grads)
    mixer_result = lax.psum_scatter(partial_value, "head", scatter_dimension=1, tiled=True)

    grad_lin, local_back = call(
        lin_kernel,
        heads,
        [col, col, turned, line],
        [col, st],
        [large((rows, width), BF16), shape((heads, DH, DH), BF16)],
        flops=mm // 4,
        size=3 << 20,
    )(queries, grad_mixed, normed, inverse)
    local_back, g_far = lax.optimization_barrier((local_back, grad_mixed))
    edge_grad = large((edge, width), BF16)
    dq_far, far_k, far_v, delta = call(
        far_kernel,
        heads,
        [col, col, col, col, tri, turned],
        [turned, columns(edge), columns(edge), line],
        [flat_t, edge_grad, edge_grad, shape((heads, 1, rows), F32)],
        scratch=[pltpu.VMEM((rows, rows), BF16)],
        flops=8 * mm // 8,
        size=8 << 20,
    )(queries, g_far, kh, vh, far, window)
    back_k, back_v = shifted(far_k, -1), shifted(far_v, -1)

    later, grad_lin, _ = carry_states(local_back, True, grad_lin)

    total = parts[0].astype(F32)
    for by in range(1, ZS):
        total = total + hop_z(parts[by], by).astype(F32)
    projection_sensitivity = total * tokens_all ** (-0.5)

    grad_queries, near_k, near_v = call(
        near_kernel,
        heads,
        [col, col, col, col, col, tri, tri, st, line, turned],
        [col, col, col],
        [large((rows, width), BF16), large((rows, width), F32), large((rows, width), F32)],
        scratch=[pltpu.VMEM((rows, rows), BF16)],
        flops=12 * mm // 8,
        size=12 << 20,
    )(queries, keys, values, grad_mixed, grad_lin, near, raw, before, delta, dq_far)

    grad_keys, grad_values = call(
        last_kernel,
        heads,
        [col, col, st, col, col, columns(edge), columns(edge)],
        [col, col],
        [large((rows, width), BF16)] * 2,
        flops=mm // 2,
        size=5 << 20,
    )(keys, values, later, near_k, near_v, back_k, back_v)
    return (mixer_result, grad_queries, grad_keys, grad_values, projection_sensitivity)


def solution(mesh):
    placed = (
        P("seq", "head"),
        P("seq", "head"),
        P("seq", "head"),
        P("head", "seq"),
        P("seq", "head"),
    )
    return jax.shard_map(
        shards,
        mesh=mesh,
        in_specs=placed,
        out_specs=(
            P("seq", "head"),
            P("seq", "head"),
            P("seq", "head"),
            P("seq", "head"),
            P("head", "seq"),
        ),
        check_vma=False,
    )
```

```python
import functools
import math

import jax
import jax.numpy as jnp
from jax import lax
from jax.experimental import pallas as pl
from jax.experimental.pallas import tpu as pltpu
from jax.sharding import PartitionSpec as P

DH = 128
BLOCK = 64
BAND = 8
TILE = 128
TOK = BAND * BLOCK
EDGE = TOK - BLOCK
SCALE = 1.0 / math.sqrt(DH)
EPSILON = 1e-05
MASKED = -1e30
F32 = jnp.float32
BF16 = jnp.bfloat16


def nn(a, b):
    return lax.dot_general(a, b, (((1,), (0,)), ((), ())), preferred_element_type=F32)


def nt(a, b):
    return lax.dot_general(a, b, (((1,), (1,)), ((), ())), preferred_element_type=F32)


def tn(a, b):
    return lax.dot_general(a, b, (((0,), (0,)), ((), ())), preferred_element_type=F32)


def flip(a):
    return a.astype(F32).T


def call(kernel, heads, ins, outs, out_shape, scratch=(), flops=0, size=0, prefetch=0):
    run = pl.pallas_call(
        kernel,
        grid_spec=pltpu.PrefetchScalarGridSpec(
            num_scalar_prefetch=prefetch,
            grid=heads if isinstance(heads, tuple) else (heads,),
            in_specs=ins,
            out_specs=outs,
            scratch_shapes=scratch,
        ),
        out_shape=out_shape,
        compiler_params=pltpu.CompilerParams(
            vmem_limit_bytes=40 * 1024 * 1024
        ),
        cost_estimate=pl.CostEstimate(flops=0, bytes_accessed=0, transcendentals=0),
    )
    return lambda *args: run(*args[:prefetch], *(kept(a) for a in args[prefetch:]))


def kept(a):
    return pltpu.with_memory_space_constraint(a, pltpu.HBM)


def large(*args):
    return pltpu.HBM(*args)


def columns(rows, at=0):
    return pl.BlockSpec((rows, DH), lambda h, *_: (at, h))


def heads_of(*dims):
    return pl.BlockSpec((1,) + dims, lambda h, *_: (h,) + (0,) * len(dims))


def rows_of(rows, cols):
    return pl.BlockSpec((rows, cols), lambda h, *_: (h, 0))


def sums_kernel(k, v, out):
    out[0] = tn(k[...], v[...]).astype(BF16)


def causal_tile():
    row = lax.broadcasted_iota(jnp.int32, (TILE, TILE), 0)
    col = lax.broadcasted_iota(jnp.int32, (TILE, TILE), 1)
    return row <= col


def edge_tile():
    row = lax.broadcasted_iota(jnp.int32, (TILE, TILE), 0)
    col = lax.broadcasted_iota(jnp.int32, (TILE, TILE), 1)
    return (row >= BLOCK) & (col < BLOCK)


def window_kernel(place, q, k, v, kw, vw, near, far, raw, window, intra):
    causal, edge = causal_tile(), edge_tile()
    inside = place[0] > 0
    v_t = flip(v[...]).astype(BF16)
    vh_t = flip(vw[...]).astype(BF16)
    for i in range(TOK // TILE):
        lo, hi = i * TILE, (i + 1) * TILE
        q_i = q[lo:hi, :]
        s_near = nt(k[0:hi, :], q_i)
        s_far = nt(kw[lo:TOK, :], q_i) * SCALE
        if i == 0:
            s_near = jnp.where(causal, s_near, 0.0)
            raw_i = s_near.astype(BF16)
            s_near = jnp.where(causal, s_near * SCALE, MASKED)
        else:
            full, last = s_near[0:lo], s_near[lo:hi]
            raw_i = jnp.concatenate([full, jnp.where(causal, last, 0.0)]).astype(BF16)
            s_near = jnp.concatenate([full * SCALE, jnp.where(causal, last * SCALE, MASKED)])
        raw[0, 0:hi, lo:hi] = raw_i
        head = jnp.where(edge, s_far[0:TILE], MASKED)
        if i < TOK // TILE - 1:
            s_far = jnp.concatenate([head, s_far[TILE:]])
        else:
            s_far = head
        s_far = jnp.where(inside, s_far, MASKED)
        top = jnp.maximum(
            jnp.max(s_near, axis=0, keepdims=True), jnp.max(s_far, axis=0, keepdims=True)
        )
        p_near = jnp.exp(s_near - top)
        p_far = jnp.exp(s_far - top)
        inv = 1.0 / (
            jnp.sum(p_near, axis=0, keepdims=True) + jnp.sum(p_far, axis=0, keepdims=True)
        )
        p_near = (p_near * inv).astype(BF16)
        p_far = (p_far * inv).astype(BF16)
        near[0, 0:hi, lo:hi] = p_near
        far[0, lo:TOK, lo:hi] = p_far
        window[:, lo:hi] = nn(v_t[:, 0:hi], p_near) + nn(vh_t[:, lo:TOK], p_far)
        intra[:, lo:hi] = nn(v_t[:, 0:hi], raw_i)


def mixed_kernel(q, before, window, intra, normed, inverse, mixed_t, mixed):
    lin = intra[...] + nt(flip(before[0]).astype(BF16), q[...])
    inv = lax.rsqrt(jnp.mean(lin * lin, axis=0, keepdims=True) + EPSILON)
    unit = lin * inv
    normed[...] = unit
    inverse[0] = inv
    out = unit + window[...]
    mixed_t[...] = out.astype(BF16)
    mixed[...] = out.T.astype(BF16)


def far_kernel(q, g, kw, vw, far, window, dq, back, delta, ds):
    g_t = flip(g[...])
    d = jnp.sum(g_t * window[...], axis=0, keepdims=True)
    delta[0] = d
    kh_t = flip(kw[...]).astype(BF16)
    for i in range(TOK // TILE):
        lo, hi = i * TILE, (i + 1) * TILE
        dp = nt(vw[lo:TOK, :], g[lo:hi, :])
        part = (far[0, lo:TOK, lo:hi].astype(F32) * (dp - d[:, lo:hi]) * SCALE).astype(BF16)
        ds[lo:TOK, lo:hi] = part
        dq[:, lo:hi] = nn(kh_t[:, lo:TOK], part)
    for j in range(TOK // TILE):
        lo, hi = j * TILE, (j + 1) * TILE
        dk_j = nn(ds[lo:hi, 0:hi], q[0:hi, :]).astype(BF16)
        dv_j = nn(far[0, lo:hi, 0:hi], g[0:hi, :]).astype(BF16)
        if j == 0:
            back[0 : hi - BLOCK, :] = dk_j[BLOCK:]
            back[EDGE : EDGE + hi - BLOCK, :] = dv_j[BLOCK:]
        else:
            back[lo - BLOCK : hi - BLOCK, :] = dk_j
            back[EDGE + lo - BLOCK : EDGE + hi - BLOCK, :] = dv_j


def lin_kernel(q, g, normed, inverse, grad_lin, sums):
    g_t = flip(g[...])
    unit = normed[...]
    inner = jnp.mean(g_t * unit, axis=0, keepdims=True)
    out = inverse[0] * (g_t - unit * inner)
    rows = out.T.astype(BF16)
    grad_lin[...] = rows
    sums[0] = tn(q[...], rows).astype(BF16)


def near_kernel(q, k, v, g, gl, near, raw, before, delta, dq_far, dq, dk, dv, both):
    causal = causal_tile()
    d = delta[0]
    k_t = flip(k[...]).astype(BF16)
    dq_t = dq_far[...] + nt(before[0], gl[...])
    parts = []
    for i in range(TOK // TILE):
        lo, hi = i * TILE, (i + 1) * TILE
        dp = nt(v[0:hi, :], g[lo:hi, :])
        ig = nt(v[0:hi, :], gl[lo:hi, :])
        last = jnp.where(causal, ig[lo:hi], 0.0)
        ig = last if i == 0 else jnp.concatenate([ig[0:lo], last])
        sum_i = near[0, 0:hi, lo:hi].astype(F32) * (dp - d[:, lo:hi]) * SCALE + ig
        sum_i = sum_i.astype(BF16)
        both[0:hi, lo:hi] = sum_i
        parts.append(dq_t[:, lo:hi] + nn(k_t[:, 0:hi], sum_i))
    dq[...] = jnp.concatenate(parts, axis=1).T.astype(BF16)
    for j in range(TOK // TILE):
        lo, hi = j * TILE, (j + 1) * TILE
        dk[lo:hi, :] = nn(both[lo:hi, lo:TOK], q[lo:TOK, :])
        dv[lo:hi, :] = nn(near[0, lo:hi, lo:TOK], g[lo:TOK, :]) + nn(
            raw[0, lo:hi, lo:TOK], gl[lo:TOK, :]
        )


def last_kernel(k, v, later, dk, dv, rk, rv, out_k, out_v):
    state = later[0]
    add_k = dk[...] + nt(v[...], state)
    add_v = dv[...] + nn(k[...], state)
    out_k[0:BLOCK, :] = add_k[0:BLOCK].astype(BF16)
    out_v[0:BLOCK, :] = add_v[0:BLOCK].astype(BF16)
    out_k[BLOCK:TOK, :] = (add_k[BLOCK:] + rk[...].astype(F32)).astype(BF16)
    out_v[BLOCK:TOK, :] = (add_v[BLOCK:] + rv[...].astype(F32)).astype(BF16)


def scan_kernel(backward, x, out):
    total = jnp.zeros(x.shape[1:], F32)
    count = x.shape[0]
    for i in range(count):
        at = count - 1 - i if backward else i
        out[at] = total.astype(BF16)
        total = total + x[at].astype(F32)


def carry_states(local, backward, beside=(), between=()):
    count = lax.axis_size("seq")
    pieces = local.reshape(count, -1, DH)
    met = lax.all_to_all(pieces, "seq", 0, 0)
    met, between = lax.optimization_barrier((met, between))
    done = pl.pallas_call(
        functools.partial(scan_kernel, backward),
        out_shape=jax.ShapeDtypeStruct(met.shape, BF16),
    )(met)
    done, beside = lax.optimization_barrier((done, beside))
    return lax.all_to_all(done, "seq", 0, 0).reshape(local.shape), beside, between


def block_id(t, head):
    x = (head[0] // 2 + XS - t % XS) % XS
    core = jnp.where(t < XS, head[0] % 2, 1 - head[0] % 2)
    return 2 * x + core


def project_kernel(head, mixed, w, *refs):
    blocks, (partial_value, out, acc) = refs[:-3], refs[-3:]
    t = pl.program_id(0)

    @pl.when(t == 0)
    def _():
        acc[...] = jnp.zeros_like(acc)

    partial_value[...] = nn(mixed[...], w[...]).astype(BF16)
    for j, block in enumerate(blocks):

        @pl.when(t == j)
        def _(block=block):
            acc[...] += nt(block[...], w[...])

    @pl.when(t == len(blocks) - 1)
    def _():
        out[...] = acc[...].astype(BF16)


def sens_kernel(place, mine, other, *refs):
    sources, outs, acc = refs[:YS], refs[YS:-1], refs[-1]
    side, turn = pl.program_id(0), pl.program_id(1)
    half = jnp.where(side == 0, place[2], 1 - place[2])

    @pl.when(turn == 0)
    def _():
        acc[...] = jnp.zeros_like(acc)

    for r, source in enumerate(sources):

        @pl.when((turn == r) & (side == 0))
        def _(source=source):
            acc[...] += nn(source[...], mine[0])

        @pl.when((turn == r) & (side == 1))
        def _(source=source):
            acc[...] += nn(source[...], other[0])

    @pl.when(turn == YS - 1)
    def _():
        count = ZS // 2
        for i in range(count):
            slot = (half * count + i + ZS - place[1]) % ZS
            part = acc[:, i * DH : (i + 1) * DH].astype(BF16)
            for r, out in enumerate(outs):

                @pl.when(slot == r)
                def _(out=out, part=part):
                    out[...] = part


YS, ZS, XS = 4, 8, 4
Y_HOPS = (1, YS - 1, 2)


def shifted(shard, by):
    count = lax.axis_size("seq")
    pairs = [(i, i + by) for i in range(count) if 0 <= i + by < count]
    return lax.ppermute(shard, "seq", pairs)


Z_GROUPS = [[y * ZS + z for z in range(ZS)] for y in range(YS)]
Y_GROUPS = [[y * ZS + z for y in range(YS)] for z in range(ZS)]


def exchange(pieces, axis, groups):
    return lax.all_to_all(pieces, axis, 0, 0, axis_index_groups=groups)


def spread(shard, axis, groups):
    copies = jnp.broadcast_to(shard[None], (len(groups[0]),) + shard.shape)
    return exchange(copies, axis, groups)


def hop_y(shard, by):
    return lax.ppermute(
        shard, "seq", [(y * ZS + z, (y + by) % YS * ZS + z) for y in range(YS) for z in range(ZS)]
    )


X_GROUPS = [[2 * x + c for x in range(XS)] for c in range(2)]


def hop_x(shard, by):
    return lax.ppermute(
        shard, "head", [(x * 2 + c, (x + by) % XS * 2 + c) for x in range(XS) for c in range(2)]
    )


def swap_core(shard):
    return lax.ppermute(shard, "head", [(i, i ^ 1) for i in range(2 * XS)])


def hop_z(shard, by):
    return lax.ppermute(
        shard, "seq", [(y * ZS + z, y * ZS + (z + by) % ZS) for y in range(YS) for z in range(ZS)]
    )


def turn_xy(shard):
    pairs = [
        ((y * ZS + z) * 2 * XS + 2 * x + c, (x * ZS + z) * 2 * XS + 2 * y + c)
        for y in range(YS)
        for z in range(ZS)
        for x in range(XS)
        for c in range(2)
    ]
    return lax.ppermute(shard, ("seq", "head"), pairs)


def shards(queries, keys, values, w_out, grad_y):
    rows, width = queries.shape
    heads = width // DH
    seq = lax.axis_index("seq").reshape(1).astype(jnp.int32)
    tokens_all = rows * lax.axis_size("seq")
    shape = jax.ShapeDtypeStruct
    col = columns(rows)
    tri = heads_of(rows, rows)
    st = heads_of(DH, DH)
    turned = rows_of(DH, rows)
    line = heads_of(1, rows)
    mm = 2 * rows * rows * width

    head = lax.axis_index("head").reshape(1).astype(jnp.int32)
    place = jnp.concatenate([seq // ZS, seq % ZS, head % 2])

    full_w = lax.all_gather(w_out, "seq", axis=1, tiled=True)
    hopped = [hop_x(grad_y, by) for by in range(1, XS)]
    local = call(
        sums_kernel, heads, [col, col], st, shape((heads, DH, DH), BF16), flops=2 * mm // 4
    )(keys, values)
    local, k_out, v_out = lax.optimization_barrier((local, keys, values))
    kh, vh = shifted(k_out, 1), shifted(v_out, 1)
    before, (grad_out, kh, vh, hopped), _ = carry_states(local, False, (grad_y, kh, vh, hopped))
    turned_grad = turn_xy(grad_out)

    sq = large((heads, rows, rows), BF16)
    flat_t = large((width, rows), F32)
    edge = EDGE
    near, far, raw, window, intra = call(
        window_kernel,
        heads,
        [col] * 5,
        [tri, tri, tri, turned, turned],
        [sq, sq, sq, flat_t, flat_t],
        flops=12 * mm // 8,
        size=12 << 20,
        prefetch=1,
    )(seq, queries, keys, values, kh, vh)

    before, window, turned_grad = lax.optimization_barrier((before, window, turned_grad))
    mine = spread(turned_grad, "head", X_GROUPS)
    normed, inverse, mixed_t, mixed = call(
        mixed_kernel,
        heads,
        [col, st, turned, turned],
        [turned, line, turned, col],
        [
            flat_t,
            shape((heads, 1, rows), F32),
            large((width, rows), BF16),
            large((rows, width), BF16),
        ],
        flops=mm // 4,
        size=5 << 20,
    )(queries, before, window, intra)

    hopped, mixed_t = lax.optimization_barrier((hopped, mixed_t))
    across_y = [mixed_t] + [hop_y(mixed_t, by) for by in range(1, YS)]
    mine, across_y = lax.optimization_barrier((mine, across_y))
    grads = [grad_y] + hopped
    grads = grads + [swap_core(g) for g in grads]
    other = swap_core(mine)
    fixed = pl.BlockSpec((rows, width), lambda *_: (0, 0))
    parts = call(
        sens_kernel,
        (2, YS),
        [
            pl.BlockSpec(
                (1, rows, width),
                lambda s, by, place: (
                    jnp.where(s == 0, (place[0] + YS - by) % YS, (place[0] + 1) % YS), 0, 0
                ),
            ),
            pl.BlockSpec(
                (1, rows, width),
                lambda s, by, place: (
                    jnp.where(s == 1, (place[0] + YS - by) % YS, place[0] % YS), 0, 0
                ),
            ),
        ]
        + [fixed] * YS,
        [pl.BlockSpec((width, DH), lambda *_: (0, 0))] * ZS,
        [large((width, DH), BF16)] * ZS,
        scratch=[pltpu.VMEM((width, rows), F32)],
        prefetch=1,
    )(place, mine, other, *across_y)
    parts, full_w = lax.optimization_barrier((parts, full_w))
    by_block = pl.BlockSpec((rows, width), lambda t, head: (0, block_id(t, head)))
    partial_value, grad_mixed = call(
        project_kernel,
        2 * XS,
        [fixed, by_block] + [fixed] * (2 * XS),
        [by_block, fixed],
        [large((rows, 2 * XS * width), BF16), large((rows, width), BF16)],
        scratch=[pltpu.VMEM((rows, width), F32)],
        prefetch=1,
    )(head, mixed, full_w, *grads)
    mixer_result = lax.psum_scatter(partial_value, "head", scatter_dimension=1, tiled=True)

    grad_lin, local_back = call(
        lin_kernel,
        heads,
        [col, col, turned, line],
        [col, st],
        [large((rows, width), BF16), shape((heads, DH, DH), BF16)],
        flops=mm // 4,
        size=3 << 20,
    )(queries, grad_mixed, normed, inverse)
    local_back, g_far = lax.optimization_barrier((local_back, grad_mixed))
    dq_far, back, delta = call(
        far_kernel,
        heads,
        [col, col, col, col, tri, turned],
        [turned, columns(2 * edge), line],
        [flat_t, large((2 * edge, width), BF16), shape((heads, 1, rows), F32)],
        scratch=[pltpu.VMEM((rows, rows), BF16)],
        flops=8 * mm // 8,
        size=8 << 20,
    )(queries, g_far, kh, vh, far, window)
    back = shifted(back, -1)

    parts, local_back = lax.optimization_barrier((parts, local_back))
    sums = [parts[0]] + [hop_z(parts[by], by) for by in range(1, ZS)]
    later, grad_lin, _ = carry_states(local_back, True, grad_lin)


    grad_queries, near_k, near_v = call(
        near_kernel,
        heads,
        [col, col, col, col, col, tri, tri, st, line, turned],
        [col, col, col],
        [large((rows, width), BF16), large((rows, width), F32), large((rows, width), F32)],
        scratch=[pltpu.VMEM((rows, rows), BF16)],
        flops=12 * mm // 8,
        size=12 << 20,
    )(queries, keys, values, grad_mixed, grad_lin, near, raw, before, delta, dq_far)

    grad_keys, grad_values = call(
        last_kernel,
        heads,
        [col, col, st, col, col, columns(edge), columns(edge, 1)],
        [col, col],
        [large((rows, width), BF16)] * 2,
        flops=mm // 2,
        size=5 << 20,
    )(keys, values, later, near_k, near_v, back, back)
    sums, grad_keys = lax.optimization_barrier((sums, grad_keys))
    total = sum(part.astype(F32) for part in sums)
    projection_sensitivity = total * tokens_all ** (-0.5)
    return (mixer_result, grad_queries, grad_keys, grad_values, projection_sensitivity)


def solution(mesh):
    placed = (
        P("seq", "head"),
        P("seq", "head"),
        P("seq", "head"),
        P("head", "seq"),
        P("seq", "head"),
    )
    return jax.shard_map(
        shards,
        mesh=mesh,
        in_specs=placed,
        out_specs=(
            P("seq", "head"),
            P("seq", "head"),
            P("seq", "head"),
            P("seq", "head"),
            P("head", "seq"),
        ),
        check_vma=False,
    )
```

```python
import functools
import math

import jax
import jax.numpy as jnp
from jax import lax
from jax.experimental import pallas as pl
from jax.experimental.pallas import tpu as pltpu
from jax.sharding import PartitionSpec as P

DH = 128
BLOCK = 64
BAND = 8
TILE = 128
TOK = BAND * BLOCK
EDGE = TOK - BLOCK
SCALE = 1.0 / math.sqrt(DH)
EPSILON = 1e-05
MASKED = -1e30
F32 = jnp.float32
BF16 = jnp.bfloat16


def nn(a, b):
    return lax.dot_general(a, b, (((1,), (0,)), ((), ())), preferred_element_type=F32)


def nt(a, b):
    return lax.dot_general(a, b, (((1,), (1,)), ((), ())), preferred_element_type=F32)


def tn(a, b):
    return lax.dot_general(a, b, (((0,), (0,)), ((), ())), preferred_element_type=F32)


def flip(a):
    return a.astype(F32).T


def call(kernel, heads, ins, outs, out_shape, scratch=(), flops=0, size=0, prefetch=0):
    run = pl.pallas_call(
        kernel,
        grid_spec=pltpu.PrefetchScalarGridSpec(
            num_scalar_prefetch=prefetch,
            grid=heads if isinstance(heads, tuple) else (heads,),
            in_specs=ins,
            out_specs=outs,
            scratch_shapes=scratch,
        ),
        out_shape=out_shape,
        compiler_params=pltpu.CompilerParams(
            vmem_limit_bytes=40 * 1024 * 1024
        ),
        cost_estimate=pl.CostEstimate(flops=0, bytes_accessed=0, transcendentals=0),
    )
    return lambda *args: run(*args[:prefetch], *(kept(a) for a in args[prefetch:]))


def kept(a):
    return pltpu.with_memory_space_constraint(a, pltpu.HBM)


def large(*args):
    return pltpu.HBM(*args)


def columns(rows, at=0):
    return pl.BlockSpec((rows, DH), lambda h, *_: (at, h))


def heads_of(*dims):
    return pl.BlockSpec((1,) + dims, lambda h, *_: (h,) + (0,) * len(dims))


def rows_of(rows, cols):
    return pl.BlockSpec((rows, cols), lambda h, *_: (h, 0))


def sums_kernel(k, v, out):
    out[0] = tn(k[...], v[...]).astype(BF16)


def causal_tile():
    row = lax.broadcasted_iota(jnp.int32, (TILE, TILE), 0)
    col = lax.broadcasted_iota(jnp.int32, (TILE, TILE), 1)
    return row <= col


def edge_tile():
    row = lax.broadcasted_iota(jnp.int32, (TILE, TILE), 0)
    col = lax.broadcasted_iota(jnp.int32, (TILE, TILE), 1)
    return (row >= BLOCK) & (col < BLOCK)


def window_kernel(place, q, k, v, kw, vw, near, far, raw, window, intra):
    causal, edge = causal_tile(), edge_tile()
    inside = place[0] > 0
    v_t = flip(v[...]).astype(BF16)
    vh_t = flip(vw[...]).astype(BF16)
    for i in range(TOK // TILE):
        lo, hi = i * TILE, (i + 1) * TILE
        q_i = q[lo:hi, :]
        s_near = nt(k[0:hi, :], q_i)
        s_far = nt(kw[lo:TOK, :], q_i) * SCALE
        if i == 0:
            s_near = jnp.where(causal, s_near, 0.0)
            raw_i = s_near.astype(BF16)
            s_near = jnp.where(causal, s_near * SCALE, MASKED)
        else:
            full, last = s_near[0:lo], s_near[lo:hi]
            raw_i = jnp.concatenate([full, jnp.where(causal, last, 0.0)]).astype(BF16)
            s_near = jnp.concatenate([full * SCALE, jnp.where(causal, last * SCALE, MASKED)])
        raw[0, 0:hi, lo:hi] = raw_i
        head = jnp.where(edge, s_far[0:TILE], MASKED)
        if i < TOK // TILE - 1:
            s_far = jnp.concatenate([head, s_far[TILE:]])
        else:
            s_far = head
        s_far = jnp.where(inside, s_far, MASKED)
        top = jnp.maximum(
            jnp.max(s_near, axis=0, keepdims=True), jnp.max(s_far, axis=0, keepdims=True)
        )
        p_near = jnp.exp(s_near - top)
        p_far = jnp.exp(s_far - top)
        inv = 1.0 / (
            jnp.sum(p_near, axis=0, keepdims=True) + jnp.sum(p_far, axis=0, keepdims=True)
        )
        p_near = (p_near * inv).astype(BF16)
        p_far = (p_far * inv).astype(BF16)
        near[0, 0:hi, lo:hi] = p_near
        far[0, lo:TOK, lo:hi] = p_far
        window[:, lo:hi] = nn(v_t[:, 0:hi], p_near) + nn(vh_t[:, lo:TOK], p_far)
        intra[:, lo:hi] = nn(v_t[:, 0:hi], raw_i)


def mixed_kernel(q, before, window, intra, normed, inverse, mixed_t, mixed):
    lin = intra[...] + nt(flip(before[0]).astype(BF16), q[...])
    inv = lax.rsqrt(jnp.mean(lin * lin, axis=0, keepdims=True) + EPSILON)
    unit = lin * inv
    normed[...] = unit
    inverse[0] = inv
    out = unit + window[...]
    mixed_t[...] = out.astype(BF16)
    mixed[...] = out.T.astype(BF16)


def far_kernel(q, g, kw, vw, far, window, dq, back, delta, ds):
    g_t = flip(g[...])
    d = jnp.sum(g_t * window[...], axis=0, keepdims=True)
    delta[0] = d
    kh_t = flip(kw[...]).astype(BF16)
    for i in range(TOK // TILE):
        lo, hi = i * TILE, (i + 1) * TILE
        dp = nt(vw[lo:TOK, :], g[lo:hi, :])
        part = (far[0, lo:TOK, lo:hi].astype(F32) * (dp - d[:, lo:hi]) * SCALE).astype(BF16)
        ds[lo:TOK, lo:hi] = part
        dq[:, lo:hi] = nn(kh_t[:, lo:TOK], part)
    for j in range(TOK // TILE):
        lo, hi = j * TILE, (j + 1) * TILE
        dk_j = nn(ds[lo:hi, 0:hi], q[0:hi, :]).astype(BF16)
        dv_j = nn(far[0, lo:hi, 0:hi], g[0:hi, :]).astype(BF16)
        if j == 0:
            back[0 : hi - BLOCK, :] = dk_j[BLOCK:]
            back[EDGE : EDGE + hi - BLOCK, :] = dv_j[BLOCK:]
        else:
            back[lo - BLOCK : hi - BLOCK, :] = dk_j
            back[EDGE + lo - BLOCK : EDGE + hi - BLOCK, :] = dv_j


def lin_kernel(q, g, normed, inverse, grad_lin, sums):
    g_t = flip(g[...])
    unit = normed[...]
    inner = jnp.mean(g_t * unit, axis=0, keepdims=True)
    out = inverse[0] * (g_t - unit * inner)
    rows = out.T.astype(BF16)
    grad_lin[...] = rows
    sums[0] = tn(q[...], rows).astype(BF16)


def near_kernel(q, k, v, g, gl, near, raw, before, delta, dq_far, dq, dk, dv, both):
    causal = causal_tile()
    d = delta[0]
    k_t = flip(k[...]).astype(BF16)
    dq_t = dq_far[...] + nt(before[0], gl[...])
    parts = []
    for i in range(TOK // TILE):
        lo, hi = i * TILE, (i + 1) * TILE
        dp = nt(v[0:hi, :], g[lo:hi, :])
        ig = nt(v[0:hi, :], gl[lo:hi, :])
        last = jnp.where(causal, ig[lo:hi], 0.0)
        ig = last if i == 0 else jnp.concatenate([ig[0:lo], last])
        sum_i = near[0, 0:hi, lo:hi].astype(F32) * (dp - d[:, lo:hi]) * SCALE + ig
        sum_i = sum_i.astype(BF16)
        both[0:hi, lo:hi] = sum_i
        parts.append(dq_t[:, lo:hi] + nn(k_t[:, 0:hi], sum_i))
    dq[...] = jnp.concatenate(parts, axis=1).T.astype(BF16)
    for j in range(TOK // TILE):
        lo, hi = j * TILE, (j + 1) * TILE
        dk[lo:hi, :] = nn(both[lo:hi, lo:TOK], q[lo:TOK, :])
        dv[lo:hi, :] = nn(near[0, lo:hi, lo:TOK], g[lo:TOK, :]) + nn(
            raw[0, lo:hi, lo:TOK], gl[lo:TOK, :]
        )


def last_kernel(k, v, later, dk, dv, rk, rv, out_k, out_v):
    state = later[0]
    add_k = dk[...] + nt(v[...], state)
    add_v = dv[...] + nn(k[...], state)
    out_k[0:BLOCK, :] = add_k[0:BLOCK].astype(BF16)
    out_v[0:BLOCK, :] = add_v[0:BLOCK].astype(BF16)
    out_k[BLOCK:TOK, :] = (add_k[BLOCK:] + rk[...].astype(F32)).astype(BF16)
    out_v[BLOCK:TOK, :] = (add_v[BLOCK:] + rv[...].astype(F32)).astype(BF16)


def scan_kernel(backward, x, out):
    total = jnp.zeros(x.shape[1:], F32)
    count = x.shape[0]
    for i in range(count):
        at = count - 1 - i if backward else i
        out[at] = total.astype(BF16)
        total = total + x[at].astype(F32)


def carry_states(local, backward, beside=(), between=()):
    count = lax.axis_size("seq")
    pieces = local.reshape(count, -1, DH)
    met = lax.all_to_all(pieces, "seq", 0, 0)
    met, between = lax.optimization_barrier((met, between))
    done = pl.pallas_call(
        functools.partial(scan_kernel, backward),
        out_shape=jax.ShapeDtypeStruct(met.shape, BF16),
    )(met)
    done, beside = lax.optimization_barrier((done, beside))
    return lax.all_to_all(done, "seq", 0, 0).reshape(local.shape), beside, between


def block_id(t, head):
    x = (head[0] // 2 + XS - t % XS) % XS
    core = jnp.where(t < XS, head[0] % 2, 1 - head[0] % 2)
    return 2 * x + core


def project_kernel(head, mixed, w, *refs):
    blocks, (partial_value, out, acc) = refs[:-3], refs[-3:]
    t = pl.program_id(0)

    @pl.when(t == 0)
    def _():
        acc[...] = jnp.zeros_like(acc)

    partial_value[...] = nn(mixed[...], w[...]).astype(BF16)
    for j, block in enumerate(blocks):

        @pl.when(t == j)
        def _(block=block):
            acc[...] += nt(block[...], w[...])

    @pl.when(t == len(blocks) - 1)
    def _():
        out[...] = acc[...].astype(BF16)


def sens_kernel(place, mine, other, *refs):
    sources, outs, acc = refs[:YS], refs[YS:-1], refs[-1]
    side, turn = pl.program_id(0), pl.program_id(1)
    half = jnp.where(side == 0, place[2], 1 - place[2])

    @pl.when(turn == 0)
    def _():
        acc[...] = jnp.zeros_like(acc)

    for r, source in enumerate(sources):

        @pl.when((turn == r) & (side == 0))
        def _(source=source):
            acc[...] += nn(source[...], mine[0])

        @pl.when((turn == r) & (side == 1))
        def _(source=source):
            acc[...] += nn(source[...], other[0])

    @pl.when(turn == YS - 1)
    def _():
        count = ZS // 2
        for i in range(count):
            slot = (half * count + i + ZS - place[1]) % ZS
            part = acc[:, i * DH : (i + 1) * DH].astype(BF16)
            for r, out in enumerate(outs):

                @pl.when(slot == r)
                def _(out=out, part=part):
                    out[...] = part


YS, ZS, XS = 4, 8, 4
Y_HOPS = (1, YS - 1, 2)


def shifted(shard, by):
    count = lax.axis_size("seq")
    pairs = [(i, i + by) for i in range(count) if 0 <= i + by < count]
    return lax.ppermute(shard, "seq", pairs)


Z_GROUPS = [[y * ZS + z for z in range(ZS)] for y in range(YS)]
Y_GROUPS = [[y * ZS + z for y in range(YS)] for z in range(ZS)]


def exchange(pieces, axis, groups):
    return lax.all_to_all(pieces, axis, 0, 0, axis_index_groups=groups)


def spread(shard, axis, groups):
    copies = jnp.broadcast_to(shard[None], (len(groups[0]),) + shard.shape)
    return exchange(copies, axis, groups)


def hop_y(shard, by):
    return lax.ppermute(
        shard, "seq", [(y * ZS + z, (y + by) % YS * ZS + z) for y in range(YS) for z in range(ZS)]
    )


X_GROUPS = [[2 * x + c for x in range(XS)] for c in range(2)]


def hop_x(shard, by):
    return lax.ppermute(
        shard, "head", [(x * 2 + c, (x + by) % XS * 2 + c) for x in range(XS) for c in range(2)]
    )


def swap_core(shard):
    return lax.ppermute(shard, "head", [(i, i ^ 1) for i in range(2 * XS)])


def hop_z(shard, by):
    return lax.ppermute(
        shard, "seq", [(y * ZS + z, y * ZS + (z + by) % ZS) for y in range(YS) for z in range(ZS)]
    )


def turn_xy(shard):
    pairs = [
        ((y * ZS + z) * 2 * XS + 2 * x + c, (x * ZS + z) * 2 * XS + 2 * y + c)
        for y in range(YS)
        for z in range(ZS)
        for x in range(XS)
        for c in range(2)
    ]
    return lax.ppermute(shard, ("seq", "head"), pairs)


def shards(queries, keys, values, w_out, grad_y):
    rows, width = queries.shape
    heads = width // DH
    seq = lax.axis_index("seq").reshape(1).astype(jnp.int32)
    tokens_all = rows * lax.axis_size("seq")
    shape = jax.ShapeDtypeStruct
    col = columns(rows)
    tri = heads_of(rows, rows)
    st = heads_of(DH, DH)
    turned = rows_of(DH, rows)
    line = heads_of(1, rows)
    mm = 2 * rows * rows * width

    head = lax.axis_index("head").reshape(1).astype(jnp.int32)
    place = jnp.concatenate([seq // ZS, seq % ZS, head % 2])

    full_w = lax.all_gather(w_out, "seq", axis=1, tiled=True)
    hopped = [hop_x(grad_y, by) for by in range(1, XS)]
    local = call(
        sums_kernel, heads, [col, col], st, shape((heads, DH, DH), BF16), flops=2 * mm // 4
    )(keys, values)
    local, k_out, v_out = lax.optimization_barrier((local, keys, values))
    kh, vh = shifted(k_out, 1), shifted(v_out, 1)
    before, grad_out, _ = carry_states(local, False, grad_y)
    turned_grad = turn_xy(grad_out)

    sq = large((heads, rows, rows), BF16)
    flat_t = large((width, rows), F32)
    edge = EDGE
    near, far, raw, window, intra = call(
        window_kernel,
        heads,
        [col] * 5,
        [tri, tri, tri, turned, turned],
        [sq, sq, sq, flat_t, flat_t],
        flops=12 * mm // 8,
        size=12 << 20,
        prefetch=1,
    )(seq, queries, keys, values, kh, vh)

    normed, inverse, mixed_t, mixed = call(
        mixed_kernel,
        heads,
        [col, st, turned, turned],
        [turned, line, turned, col],
        [
            flat_t,
            shape((heads, 1, rows), F32),
            large((width, rows), BF16),
            large((rows, width), BF16),
        ],
        flops=mm // 4,
        size=5 << 20,
    )(queries, before, window, intra)

    turned_grad, hopped, mixed_t = lax.optimization_barrier((turned_grad, hopped, mixed_t))
    mine = spread(turned_grad, "head", X_GROUPS)
    across_y = [mixed_t] + [hop_y(mixed_t, by) for by in range(1, YS)]
    grads = [grad_y] + hopped
    grads = grads + [swap_core(g) for g in grads]
    mine, across_y = lax.optimization_barrier((mine, across_y))
    other = swap_core(mine)
    mine, other, across_y, full_w = lax.optimization_barrier((mine, other, across_y, full_w))
    fixed = pl.BlockSpec((rows, width), lambda *_: (0, 0))
    by_block = pl.BlockSpec((rows, width), lambda t, head: (0, block_id(t, head)))
    partial_value, grad_mixed = call(
        project_kernel,
        2 * XS,
        [fixed, by_block] + [fixed] * (2 * XS),
        [by_block, fixed],
        [large((rows, 2 * XS * width), BF16), large((rows, width), BF16)],
        scratch=[pltpu.VMEM((rows, width), F32)],
        prefetch=1,
    )(head, mixed, full_w, *grads)
    mixer_result = lax.psum_scatter(partial_value, "head", scatter_dimension=1, tiled=True)

    grad_lin, local_back = call(
        lin_kernel,
        heads,
        [col, col, turned, line],
        [col, st],
        [large((rows, width), BF16), shape((heads, DH, DH), BF16)],
        flops=mm // 4,
        size=3 << 20,
    )(queries, grad_mixed, normed, inverse)
    local_back, g_far = lax.optimization_barrier((local_back, grad_mixed))
    dq_far, back, delta = call(
        far_kernel,
        heads,
        [col, col, col, col, tri, turned],
        [turned, columns(2 * edge), line],
        [flat_t, large((2 * edge, width), BF16), shape((heads, 1, rows), F32)],
        scratch=[pltpu.VMEM((rows, rows), BF16)],
        flops=8 * mm // 8,
        size=8 << 20,
    )(queries, g_far, kh, vh, far, window)
    back = shifted(back, -1)

    mine, other, across_y, local_back = lax.optimization_barrier(
        (mine, other, across_y, local_back)
    )
    parts = call(
        sens_kernel,
        (2, YS),
        [
            pl.BlockSpec(
                (1, rows, width),
                lambda s, by, place: (
                    jnp.where(s == 0, (place[0] + YS - by) % YS, (place[0] + 1) % YS), 0, 0
                ),
            ),
            pl.BlockSpec(
                (1, rows, width),
                lambda s, by, place: (
                    jnp.where(s == 1, (place[0] + YS - by) % YS, place[0] % YS), 0, 0
                ),
            ),
        ]
        + [fixed] * YS,
        [pl.BlockSpec((width, DH), lambda *_: (0, 0))] * ZS,
        [large((width, DH), BF16)] * ZS,
        scratch=[pltpu.VMEM((width, rows), F32)],
        prefetch=1,
    )(place, mine, other, *across_y)
    sums = [parts[0]] + [hop_z(parts[by], by) for by in range(1, ZS)]
    later, grad_lin, _ = carry_states(local_back, True, grad_lin)


    grad_queries, near_k, near_v = call(
        near_kernel,
        heads,
        [col, col, col, col, col, tri, tri, st, line, turned],
        [col, col, col],
        [large((rows, width), BF16), large((rows, width), F32), large((rows, width), F32)],
        scratch=[pltpu.VMEM((rows, rows), BF16)],
        flops=12 * mm // 8,
        size=12 << 20,
    )(queries, keys, values, grad_mixed, grad_lin, near, raw, before, delta, dq_far)

    grad_keys, grad_values = call(
        last_kernel,
        heads,
        [col, col, st, col, col, columns(edge), columns(edge, 1)],
        [col, col],
        [large((rows, width), BF16)] * 2,
        flops=mm // 2,
        size=5 << 20,
    )(keys, values, later, near_k, near_v, back, back)
    sums, grad_keys = lax.optimization_barrier((sums, grad_keys))
    total = sum(part.astype(F32) for part in sums)
    projection_sensitivity = total * tokens_all ** (-0.5)
    return (mixer_result, grad_queries, grad_keys, grad_values, projection_sensitivity)


def solution(mesh):
    placed = (
        P("seq", "head"),
        P("seq", "head"),
        P("seq", "head"),
        P("head", "seq"),
        P("seq", "head"),
    )
    return jax.shard_map(
        shards,
        mesh=mesh,
        in_specs=placed,
        out_specs=(
            P("seq", "head"),
            P("seq", "head"),
            P("seq", "head"),
            P("seq", "head"),
            P("head", "seq"),
        ),
        check_vma=False,
    )
```

```python
import functools
import math

import jax
import jax.numpy as jnp
from jax import lax
from jax.experimental import pallas as pl
from jax.experimental.pallas import tpu as pltpu
from jax.sharding import PartitionSpec as P

DH = 128
BLOCK = 64
BAND = 8
TILE = 128
TOK = BAND * BLOCK
EDGE = TOK - BLOCK
SCALE = 1.0 / math.sqrt(DH)
EPSILON = 1e-05
MASKED = -1e30
F32 = jnp.float32
BF16 = jnp.bfloat16


def nn(a, b):
    return lax.dot_general(a, b, (((1,), (0,)), ((), ())), preferred_element_type=F32)


def nt(a, b):
    return lax.dot_general(a, b, (((1,), (1,)), ((), ())), preferred_element_type=F32)


def tn(a, b):
    return lax.dot_general(a, b, (((0,), (0,)), ((), ())), preferred_element_type=F32)


def flip(a):
    return a.astype(F32).T


def call(kernel, heads, ins, outs, out_shape, scratch=(), flops=0, size=0, prefetch=0):
    run = pl.pallas_call(
        kernel,
        grid_spec=pltpu.PrefetchScalarGridSpec(
            num_scalar_prefetch=prefetch,
            grid=heads if isinstance(heads, tuple) else (heads,),
            in_specs=ins,
            out_specs=outs,
            scratch_shapes=scratch,
        ),
        out_shape=out_shape,
        compiler_params=pltpu.CompilerParams(
            vmem_limit_bytes=40 * 1024 * 1024
        ),
        cost_estimate=pl.CostEstimate(flops=0, bytes_accessed=0, transcendentals=0),
    )
    return lambda *args: run(*args[:prefetch], *(kept(a) for a in args[prefetch:]))


def kept(a):
    return pltpu.with_memory_space_constraint(a, pltpu.HBM)


def large(*args):
    return pltpu.HBM(*args)


def columns(rows, at=0):
    return pl.BlockSpec((rows, DH), lambda h, *_: (at, h))


def heads_of(*dims):
    return pl.BlockSpec((1,) + dims, lambda h, *_: (h,) + (0,) * len(dims))


def rows_of(rows, cols):
    return pl.BlockSpec((rows, cols), lambda h, *_: (h, 0))


def sums_kernel(k, v, out):
    out[0] = tn(k[...], v[...]).astype(BF16)


def causal_tile():
    row = lax.broadcasted_iota(jnp.int32, (TILE, TILE), 0)
    col = lax.broadcasted_iota(jnp.int32, (TILE, TILE), 1)
    return row <= col


def edge_tile():
    row = lax.broadcasted_iota(jnp.int32, (TILE, TILE), 0)
    col = lax.broadcasted_iota(jnp.int32, (TILE, TILE), 1)
    return (row >= BLOCK) & (col < BLOCK)


def window_kernel(place, q, k, v, kw, vw, near, far, raw, window, intra):
    causal, edge = causal_tile(), edge_tile()
    inside = place[0] > 0
    v_t = flip(v[...]).astype(BF16)
    vh_t = flip(vw[...]).astype(BF16)
    for i in range(TOK // TILE):
        lo, hi = i * TILE, (i + 1) * TILE
        q_i = q[lo:hi, :]
        s_near = nt(k[0:hi, :], q_i)
        s_far = nt(kw[lo:TOK, :], q_i) * SCALE
        if i == 0:
            s_near = jnp.where(causal, s_near, 0.0)
            raw_i = s_near.astype(BF16)
            s_near = jnp.where(causal, s_near * SCALE, MASKED)
        else:
            full, last = s_near[0:lo], s_near[lo:hi]
            raw_i = jnp.concatenate([full, jnp.where(causal, last, 0.0)]).astype(BF16)
            s_near = jnp.concatenate([full * SCALE, jnp.where(causal, last * SCALE, MASKED)])
        raw[0, 0:hi, lo:hi] = raw_i
        head = jnp.where(edge, s_far[0:TILE], MASKED)
        if i < TOK // TILE - 1:
            s_far = jnp.concatenate([head, s_far[TILE:]])
        else:
            s_far = head
        s_far = jnp.where(inside, s_far, MASKED)
        top = jnp.maximum(
            jnp.max(s_near, axis=0, keepdims=True), jnp.max(s_far, axis=0, keepdims=True)
        )
        p_near = jnp.exp(s_near - top)
        p_far = jnp.exp(s_far - top)
        inv = 1.0 / (
            jnp.sum(p_near, axis=0, keepdims=True) + jnp.sum(p_far, axis=0, keepdims=True)
        )
        p_near = (p_near * inv).astype(BF16)
        p_far = (p_far * inv).astype(BF16)
        near[0, 0:hi, lo:hi] = p_near
        far[0, lo:TOK, lo:hi] = p_far
        window[:, lo:hi] = nn(v_t[:, 0:hi], p_near) + nn(vh_t[:, lo:TOK], p_far)
        intra[:, lo:hi] = nn(v_t[:, 0:hi], raw_i)


def mixed_kernel(q, before, window, intra, normed, inverse, mixed_t, mixed):
    lin = intra[...] + nt(flip(before[0]).astype(BF16), q[...])
    inv = lax.rsqrt(jnp.mean(lin * lin, axis=0, keepdims=True) + EPSILON)
    unit = lin * inv
    normed[...] = unit
    inverse[0] = inv
    out = unit + window[...]
    mixed_t[...] = out.astype(BF16)
    mixed[...] = out.T.astype(BF16)


def far_kernel(q, g, kw, vw, far, window, dq, back, delta, ds):
    g_t = flip(g[...])
    d = jnp.sum(g_t * window[...], axis=0, keepdims=True)
    delta[0] = d
    kh_t = flip(kw[...]).astype(BF16)
    for i in range(TOK // TILE):
        lo, hi = i * TILE, (i + 1) * TILE
        dp = nt(vw[lo:TOK, :], g[lo:hi, :])
        part = (far[0, lo:TOK, lo:hi].astype(F32) * (dp - d[:, lo:hi]) * SCALE).astype(BF16)
        ds[lo:TOK, lo:hi] = part
        dq[:, lo:hi] = nn(kh_t[:, lo:TOK], part)
    for j in range(TOK // TILE):
        lo, hi = j * TILE, (j + 1) * TILE
        dk_j = nn(ds[lo:hi, 0:hi], q[0:hi, :]).astype(BF16)
        dv_j = nn(far[0, lo:hi, 0:hi], g[0:hi, :]).astype(BF16)
        if j == 0:
            back[0 : hi - BLOCK, :] = dk_j[BLOCK:]
            back[EDGE : EDGE + hi - BLOCK, :] = dv_j[BLOCK:]
        else:
            back[lo - BLOCK : hi - BLOCK, :] = dk_j
            back[EDGE + lo - BLOCK : EDGE + hi - BLOCK, :] = dv_j


def lin_kernel(q, g, normed, inverse, grad_lin, sums):
    g_t = flip(g[...])
    unit = normed[...]
    inner = jnp.mean(g_t * unit, axis=0, keepdims=True)
    out = inverse[0] * (g_t - unit * inner)
    rows = out.T.astype(BF16)
    grad_lin[...] = rows
    sums[0] = tn(q[...], rows).astype(BF16)


def near_kernel(q, k, v, g, gl, near, raw, before, delta, dq_far, dq, dk, dv, both):
    causal = causal_tile()
    d = delta[0]
    k_t = flip(k[...]).astype(BF16)
    dq_t = dq_far[...] + nt(before[0], gl[...])
    parts = []
    for i in range(TOK // TILE):
        lo, hi = i * TILE, (i + 1) * TILE
        dp = nt(v[0:hi, :], g[lo:hi, :])
        ig = nt(v[0:hi, :], gl[lo:hi, :])
        last = jnp.where(causal, ig[lo:hi], 0.0)
        ig = last if i == 0 else jnp.concatenate([ig[0:lo], last])
        sum_i = near[0, 0:hi, lo:hi].astype(F32) * (dp - d[:, lo:hi]) * SCALE + ig
        sum_i = sum_i.astype(BF16)
        both[0:hi, lo:hi] = sum_i
        parts.append(dq_t[:, lo:hi] + nn(k_t[:, 0:hi], sum_i))
    dq[...] = jnp.concatenate(parts, axis=1).T.astype(BF16)
    for j in range(TOK // TILE):
        lo, hi = j * TILE, (j + 1) * TILE
        dk[lo:hi, :] = nn(both[lo:hi, lo:TOK], q[lo:TOK, :])
        dv[lo:hi, :] = nn(near[0, lo:hi, lo:TOK], g[lo:TOK, :]) + nn(
            raw[0, lo:hi, lo:TOK], gl[lo:TOK, :]
        )


def last_kernel(k, v, later, dk, dv, rk, rv, out_k, out_v):
    state = later[0]
    add_k = dk[...] + nt(v[...], state)
    add_v = dv[...] + nn(k[...], state)
    out_k[0:BLOCK, :] = add_k[0:BLOCK].astype(BF16)
    out_v[0:BLOCK, :] = add_v[0:BLOCK].astype(BF16)
    out_k[BLOCK:TOK, :] = (add_k[BLOCK:] + rk[...].astype(F32)).astype(BF16)
    out_v[BLOCK:TOK, :] = (add_v[BLOCK:] + rv[...].astype(F32)).astype(BF16)


def scan_kernel(backward, x, out):
    total = jnp.zeros(x.shape[1:], F32)
    count = x.shape[0]
    for i in range(count):
        at = count - 1 - i if backward else i
        out[at] = total.astype(BF16)
        total = total + x[at].astype(F32)


def carry_states(local, backward, beside=(), between=()):
    count = lax.axis_size("seq")
    pieces = local.reshape(count, -1, DH)
    met = lax.all_to_all(pieces, "seq", 0, 0)
    met, between = lax.optimization_barrier((met, between))
    done = pl.pallas_call(
        functools.partial(scan_kernel, backward),
        out_shape=jax.ShapeDtypeStruct(met.shape, BF16),
    )(met)
    done, beside = lax.optimization_barrier((done, beside))
    return lax.all_to_all(done, "seq", 0, 0).reshape(local.shape), beside, between


def block_id(t, head):
    x = (head[0] // 2 + XS - t % XS) % XS
    core = jnp.where(t < XS, head[0] % 2, 1 - head[0] % 2)
    return 2 * x + core


def project_kernel(head, mixed, w, *refs):
    blocks, (partial_value, out, acc) = refs[:-3], refs[-3:]
    t = pl.program_id(0)

    @pl.when(t == 0)
    def _():
        acc[...] = jnp.zeros_like(acc)

    partial_value[...] = nn(mixed[...], w[...]).astype(BF16)
    for j, block in enumerate(blocks):

        @pl.when(t == j)
        def _(block=block):
            acc[...] += nt(block[...], w[...])

    @pl.when(t == len(blocks) - 1)
    def _():
        out[...] = acc[...].astype(BF16)


def sens_kernel(place, mine, other, *refs):
    sources, outs, acc = refs[:YS], refs[YS:-1], refs[-1]
    side, turn = pl.program_id(0), pl.program_id(1)
    half = jnp.where(side == 0, place[2], 1 - place[2])

    @pl.when(turn == 0)
    def _():
        acc[...] = jnp.zeros_like(acc)

    for r, source in enumerate(sources):

        @pl.when((turn == r) & (side == 0))
        def _(source=source):
            acc[...] += nn(source[...], mine[0])

        @pl.when((turn == r) & (side == 1))
        def _(source=source):
            acc[...] += nn(source[...], other[0])

    @pl.when(turn == YS - 1)
    def _():
        count = ZS // 2
        for i in range(count):
            slot = (half * count + i + ZS - place[1]) % ZS
            part = acc[:, i * DH : (i + 1) * DH].astype(BF16)
            for r, out in enumerate(outs):

                @pl.when(slot == r)
                def _(out=out, part=part):
                    out[...] = part


YS, ZS, XS = 4, 8, 4
Y_HOPS = (1, YS - 1, 2)


def shifted(shard, by):
    count = lax.axis_size("seq")
    pairs = [(i, i + by) for i in range(count) if 0 <= i + by < count]
    return lax.ppermute(shard, "seq", pairs)


Z_GROUPS = [[y * ZS + z for z in range(ZS)] for y in range(YS)]
Y_GROUPS = [[y * ZS + z for y in range(YS)] for z in range(ZS)]


def exchange(pieces, axis, groups):
    return lax.all_to_all(pieces, axis, 0, 0, axis_index_groups=groups)


def spread(shard, axis, groups):
    copies = jnp.broadcast_to(shard[None], (len(groups[0]),) + shard.shape)
    return exchange(copies, axis, groups)


def hop_y(shard, by):
    return lax.ppermute(
        shard, "seq", [(y * ZS + z, (y + by) % YS * ZS + z) for y in range(YS) for z in range(ZS)]
    )


X_GROUPS = [[2 * x + c for x in range(XS)] for c in range(2)]


def hop_x(shard, by):
    return lax.ppermute(
        shard, "head", [(x * 2 + c, (x + by) % XS * 2 + c) for x in range(XS) for c in range(2)]
    )


def swap_core(shard):
    return lax.ppermute(shard, "head", [(i, i ^ 1) for i in range(2 * XS)])


def hop_z(shard, by):
    return lax.ppermute(
        shard, "seq", [(y * ZS + z, y * ZS + (z + by) % ZS) for y in range(YS) for z in range(ZS)]
    )


def turn_xy(shard):
    pairs = [
        ((y * ZS + z) * 2 * XS + 2 * x + c, (x * ZS + z) * 2 * XS + 2 * y + c)
        for y in range(YS)
        for z in range(ZS)
        for x in range(XS)
        for c in range(2)
    ]
    return lax.ppermute(shard, ("seq", "head"), pairs)


def shards(queries, keys, values, w_out, grad_y):
    rows, width = queries.shape
    heads = width // DH
    seq = lax.axis_index("seq").reshape(1).astype(jnp.int32)
    tokens_all = rows * lax.axis_size("seq")
    shape = jax.ShapeDtypeStruct
    col = columns(rows)
    tri = heads_of(rows, rows)
    st = heads_of(DH, DH)
    turned = rows_of(DH, rows)
    line = heads_of(1, rows)
    mm = 2 * rows * rows * width

    head = lax.axis_index("head").reshape(1).astype(jnp.int32)
    place = jnp.concatenate([seq // ZS, seq % ZS, head % 2])

    full_w = lax.all_gather(w_out, "seq", axis=1, tiled=True)
    hopped = [hop_x(grad_y, by) for by in range(1, XS)]
    local = call(
        sums_kernel, heads, [col, col], st, shape((heads, DH, DH), BF16), flops=2 * mm // 4
    )(keys, values)
    local, k_out, v_out = lax.optimization_barrier((local, keys, values))
    kh, vh = shifted(k_out, 1), shifted(v_out, 1)
    before, grad_out, _ = carry_states(local, False, grad_y)
    turned_grad = turn_xy(grad_out)

    sq = large((heads, rows, rows), BF16)
    flat_t = large((width, rows), F32)
    edge = EDGE
    near, far, raw, window, intra = call(
        window_kernel,
        heads,
        [col] * 5,
        [tri, tri, tri, turned, turned],
        [sq, sq, sq, flat_t, flat_t],
        flops=12 * mm // 8,
        size=12 << 20,
        prefetch=1,
    )(seq, queries, keys, values, kh, vh)

    normed, inverse, mixed_t, mixed = call(
        mixed_kernel,
        heads,
        [col, st, turned, turned],
        [turned, line, turned, col],
        [
            flat_t,
            shape((heads, 1, rows), F32),
            large((width, rows), BF16),
            large((rows, width), BF16),
        ],
        flops=mm // 4,
        size=5 << 20,
    )(queries, before, window, intra)

    turned_grad, hopped, mixed_t = lax.optimization_barrier((turned_grad, hopped, mixed_t))
    mine = spread(turned_grad, "head", X_GROUPS)
    across_y = [mixed_t] + [hop_y(mixed_t, by) for by in range(1, YS)]
    mine, first, hopped = lax.optimization_barrier((mine, grad_y, hopped))
    grads = [first] + hopped
    grads = grads + [swap_core(g) for g in grads]
    mine, across_y, full_w = lax.optimization_barrier((mine, across_y, full_w))
    other = swap_core(mine)
    fixed = pl.BlockSpec((rows, width), lambda *_: (0, 0))
    by_block = pl.BlockSpec((rows, width), lambda t, head: (0, block_id(t, head)))
    partial_value, grad_mixed = call(
        project_kernel,
        2 * XS,
        [fixed, by_block] + [fixed] * (2 * XS),
        [by_block, fixed],
        [large((rows, 2 * XS * width), BF16), large((rows, width), BF16)],
        scratch=[pltpu.VMEM((rows, width), F32)],
        prefetch=1,
    )(head, mixed, full_w, *grads)
    mixer_result = lax.psum_scatter(partial_value, "head", scatter_dimension=1, tiled=True)

    grad_lin, local_back = call(
        lin_kernel,
        heads,
        [col, col, turned, line],
        [col, st],
        [large((rows, width), BF16), shape((heads, DH, DH), BF16)],
        flops=mm // 4,
        size=3 << 20,
    )(queries, grad_mixed, normed, inverse)
    local_back, g_far = lax.optimization_barrier((local_back, grad_mixed))
    dq_far, back, delta = call(
        far_kernel,
        heads,
        [col, col, col, col, tri, turned],
        [turned, columns(2 * edge), line],
        [flat_t, large((2 * edge, width), BF16), shape((heads, 1, rows), F32)],
        scratch=[pltpu.VMEM((rows, rows), BF16)],
        flops=8 * mm // 8,
        size=8 << 20,
    )(queries, g_far, kh, vh, far, window)
    back = shifted(back, -1)

    mine, other, across_y, local_back = lax.optimization_barrier(
        (mine, other, across_y, local_back)
    )
    parts = call(
        sens_kernel,
        (2, YS),
        [
            pl.BlockSpec(
                (1, rows, width),
                lambda s, by, place: (
                    jnp.where(s == 0, (place[0] + YS - by) % YS, (place[0] + 1) % YS), 0, 0
                ),
            ),
            pl.BlockSpec(
                (1, rows, width),
                lambda s, by, place: (
                    jnp.where(s == 1, (place[0] + YS - by) % YS, place[0] % YS), 0, 0
                ),
            ),
        ]
        + [fixed] * YS,
        [pl.BlockSpec((width, DH), lambda *_: (0, 0))] * ZS,
        [large((width, DH), BF16)] * ZS,
        scratch=[pltpu.VMEM((width, rows), F32)],
        prefetch=1,
    )(place, mine, other, *across_y)
    sums = [parts[0]] + [hop_z(parts[by], by) for by in range(1, ZS)]
    later, grad_lin, _ = carry_states(local_back, True, grad_lin)


    grad_queries, near_k, near_v = call(
        near_kernel,
        heads,
        [col, col, col, col, col, tri, tri, st, line, turned],
        [col, col, col],
        [large((rows, width), BF16), large((rows, width), F32), large((rows, width), F32)],
        scratch=[pltpu.VMEM((rows, rows), BF16)],
        flops=12 * mm // 8,
        size=12 << 20,
    )(queries, keys, values, grad_mixed, grad_lin, near, raw, before, delta, dq_far)

    grad_keys, grad_values = call(
        last_kernel,
        heads,
        [col, col, st, col, col, columns(edge), columns(edge, 1)],
        [col, col],
        [large((rows, width), BF16)] * 2,
        flops=mm // 2,
        size=5 << 20,
    )(keys, values, later, near_k, near_v, back, back)
    sums, grad_keys = lax.optimization_barrier((sums, grad_keys))
    total = sum(part.astype(F32) for part in sums)
    projection_sensitivity = total * tokens_all ** (-0.5)
    return (mixer_result, grad_queries, grad_keys, grad_values, projection_sensitivity)


def solution(mesh):
    placed = (
        P("seq", "head"),
        P("seq", "head"),
        P("seq", "head"),
        P("head", "seq"),
        P("seq", "head"),
    )
    return jax.shard_map(
        shards,
        mesh=mesh,
        in_specs=placed,
        out_specs=(
            P("seq", "head"),
            P("seq", "head"),
            P("seq", "head"),
            P("seq", "head"),
            P("head", "seq"),
        ),
        check_vma=False,
    )
```
